32 devices in a mesh: dp: 4 (over y, core), code: 8 (over z, x).
Axes of the slice: x: 2, y: 2, z: 4, core: 2. Of those that a mesh axis runs over, the one named last changes fastest.
Arguments:
- cached_keys: bfloat16 [131072, 128], P(('dp', 'code')), may hold values from -128 to 128
- codebook: float32 [65536, 128], P('code'), may hold values from -4 to 4
- block_lists: int32 [256, 6], P(('dp', 'code')), may hold values from 0 to 255, as said below
- counts: int32 [256], P(('dp', 'code')), may hold values from 2 to 6, as said below
Outputs:
- codebook_out: float32 [65536, 128], P('code')
- logsum: float32 [131072], P(('dp', 'code'))
The draws below stay inside these ranges and needn't reach their ends.
Inputs may be any that keep to these rules, and one draw needn't show every extreme that they name: `block_lists`: within a row the first counts entries are distinct; entries past the count repeat the first. Owner o holds blocks o * (256 / the size of code) onward, consecutively; the key blocks of one device (aligned runs of 8 rows) name at most 1 distinct blocks of one owner, and in every draw one owner has exactly 1 named by every device. `counts`: some key block of every device lists 6 blocks.
All inputs are finite; a program needn't handle non-finite values.
Results may differ from the reference program's by a relative error of at most 0.0007.
Values sent between devices are 32-bit elements; how exact they have to be, the bound alone decides.
A program may use at most 64 MiB of HBM per device.

```python
import jax
import jax.numpy as jnp
from jax import lax

H = 128
CODES = 65536
CBLK = 256
BLOCK = 512
LIST_MAX = 6
CAP = 1
ITERS = 2
KB_DEV = 8
KBLOCKS = 256
KEYS = 131072
CBLOCKS = 256
N_CODE = 8


def shared_codebook(key):
    base = jax.random.fold_in(key, 11)
    return jnp.clip(jax.random.normal(base, (CODES, H), jnp.float32), -4.0, 4.0)


def shared_lists(key):
    base = jax.random.fold_in(key, 23)
    device_count = KBLOCKS // KB_DEV
    own_blocks = CODES // CBLK // N_CODE
    width_slots = N_CODE * CAP
    first = jax.random.randint(jax.random.fold_in(base, 1), (device_count, N_CODE), 0, own_blocks)
    stride = jax.random.randint(jax.random.fold_in(base, 2), (device_count, N_CODE), 1, max(own_blocks // CAP, 2))
    local = (first[:, :, None] + jnp.arange(CAP, dtype=jnp.int32)[None, None, :] * stride[:, :, None]) % own_blocks
    owner_ids = jnp.arange(N_CODE, dtype=jnp.int32)[None, :, None]
    block_ids = (owner_ids * own_blocks + local).reshape(device_count, width_slots)
    hot_owner = jax.random.randint(jax.random.fold_in(base, 3), (), 0, N_CODE)
    coin = jax.random.randint(jax.random.fold_in(base, 4), (device_count, N_CODE, CAP), 0, 2)
    slot_pos = jnp.arange(CAP, dtype=jnp.int32)[None, None, :]
    is_hot = owner_ids == hot_owner
    usable = jnp.where((slot_pos == 0) | is_hot, 1, coin).reshape(device_count, width_slots)
    slot_index = jnp.arange(width_slots, dtype=jnp.int32)
    noise = jax.random.randint(jax.random.fold_in(base, 5), (device_count, KB_DEV, width_slots), 0, 1 << 20)
    ranking = noise * width_slots + slot_index[None, None, :]
    ranking = jnp.where(usable[:, None, :] == 1, ranking, -1 - slot_index[None, None, :])
    hot_flat = jnp.broadcast_to(is_hot, (1, N_CODE, CAP)).reshape(1, width_slots)
    first_row = (jnp.arange(KB_DEV, dtype=jnp.int32) == 0)[None, :, None]
    ranking = ranking + jnp.where(first_row & hot_flat[:, None, :], 1 << 28, 0)
    top_slots = lax.top_k(ranking, LIST_MAX)[1]
    picked = jnp.take_along_axis(jnp.broadcast_to(block_ids[:, None, :], (device_count, KB_DEV, width_slots)), top_slots, axis=2)
    counts = jax.random.randint(jax.random.fold_in(base, 6), (device_count, KB_DEV), 2, LIST_MAX + 1)
    counts = jnp.where(jnp.arange(KB_DEV, dtype=jnp.int32)[None, :] == 1, LIST_MAX, counts)
    within = jnp.arange(LIST_MAX, dtype=jnp.int32)[None, None, :] < counts[:, :, None]
    picked = jnp.where(within, picked, picked[:, :, 0:1])
    return (picked.reshape(KBLOCKS, LIST_MAX).astype(jnp.int32), counts.reshape(KBLOCKS).astype(jnp.int32))


def draw_codebook(key, part):
    return shared_codebook(key)


def draw_block_lists(key, part):
    return shared_lists(key)[0]


def draw_counts(key, part):
    return shared_lists(key)[1]


def draw_cached_keys(key, part):
    noise = jnp.clip(jax.random.normal(jax.random.fold_in(key, 13), (KEYS, H), jnp.float32), -4.0, 4.0)
    return noise.astype(jnp.bfloat16)


def setup_inputs(seed: int = 0) -> dict:
    splits = jax.random.split(jax.random.key(seed), 5)
    return {
        "cached_keys": draw_cached_keys(jax.random.fold_in(splits[4], 71), 0),
        "codebook": draw_codebook(jax.random.fold_in(splits[4], 71), 0),
        "block_lists": draw_block_lists(jax.random.fold_in(splits[4], 71), 0),
        "counts": draw_counts(jax.random.fold_in(splits[4], 71), 0),
    }


def reference(cached_keys, codebook, block_lists, counts):
    masked_score = -1e+30
    key_tiles = cached_keys.reshape(-1, BLOCK, H)
    listed_ok = jnp.arange(LIST_MAX)[None, :] < counts[:, None]
    current = codebook
    logsum = None
    for sweep in range(ITERS):
        code_full = current.reshape(CBLOCKS, CBLK, H)
        code_norm = lax.optimization_barrier(jnp.sum(current * current, axis=1)).reshape(CBLOCKS, CBLK)

        def one_block(running, block_item):
            total_sums, total_mass = running
            tile_keys, picked, listed = block_item
            word_rows = code_full[picked].reshape(-1, H)
            word_norms = code_norm[picked].reshape(-1)
            inner = lax.dot_general(tile_keys.astype(jnp.float32), word_rows, (((1,), (1,)), ((), ())), precision=lax.Precision.HIGHEST, preferred_element_type=jnp.float32)
            scores = (inner - 0.5 * word_norms[None, :]) / jnp.sqrt(jnp.float32(H))
            column_live = jnp.repeat(listed, CBLK)
            scores = jnp.where(column_live[None, :], scores, masked_score)
            row_top = lax.optimization_barrier(jnp.max(scores, axis=1, keepdims=True))
            unnorm = jnp.exp(scores - row_top)
            row_total = lax.optimization_barrier(jnp.sum(unnorm, axis=1, keepdims=True))
            row_logsum = row_top[:, 0] + jnp.log(row_total[:, 0])
            posterior = (unnorm / row_total).astype(jnp.bfloat16)
            weighted = lax.dot_general(posterior, tile_keys, (((0,), (0,)), ((), ())), preferred_element_type=jnp.float32)
            weight = lax.optimization_barrier(jnp.sum(posterior.astype(jnp.float32), axis=0))
            total_sums = total_sums.at[picked].add(weighted.reshape(LIST_MAX, CBLK, H))
            total_mass = total_mass.at[picked].add(weight.reshape(LIST_MAX, CBLK))
            return ((total_sums, total_mass), row_logsum)
        start_state = (jnp.zeros((CBLOCKS, CBLK, H), jnp.float32), jnp.zeros((CBLOCKS, CBLK), jnp.float32))
        (total_sums, total_mass), logsum = lax.scan(one_block, start_state, (key_tiles, block_lists, listed_ok))
        current = (total_sums.reshape(CODES, H) + current) / (total_mass.reshape(CODES)[:, None] + 1.0)
    return (current, logsum.reshape(-1))
```

```python
import functools
import math

import jax
import jax.numpy as jnp
from jax import lax
from jax.experimental import pallas as pl
from jax.experimental.pallas import tpu as pltpu
from jax.sharding import PartitionSpec as P

CBLK = 256
LIST_MAX = 6
ITERS = 2
MROWS = 8
MESH = pl.DeviceIdType.MESH
VLIMIT = 60 * 1024 * 1024

VM = pl.BlockSpec(memory_space=pltpu.VMEM)
SM = pl.BlockSpec(memory_space=pltpu.SMEM)


def ids_kernel(n_dp, n_code, want_ref, all_ref, send_sem, recv_sem):
    n = n_dp * n_code
    me = lax.axis_index("dp") * n_code + lax.axis_index("code")
    barrier = pltpu.get_barrier_semaphore()

    def greet(k, c):
        peer = (me + k) % n
        pl.semaphore_signal(
            barrier, inc=1, device_id=(peer // n_code, peer % n_code), device_id_type=MESH
        )
        return c

    lax.fori_loop(1, n, greet, 0)
    all_ref[me] = want_ref[...]
    pl.semaphore_wait(barrier, n - 1)

    def copy(k):
        peer = (me + k) % n
        return pltpu.make_async_remote_copy(
            src_ref=want_ref,
            dst_ref=all_ref.at[me],
            send_sem=send_sem.at[k],
            recv_sem=recv_sem.at[k],
            device_id=(peer // n_code, peer % n_code),
            device_id_type=MESH,
        )

    def start(k, c):
        copy(k).start()
        return c

    lax.fori_loop(1, n, start, 0)

    def finish(k, c):
        copy(k).wait()
        return c

    lax.fori_loop(1, n, finish, 0)


def fetch_kernel(n_code, ids_ref, book_ref, out_ref, stage, send_sem, recv_sem):
    d = lax.axis_index("dp")
    o = lax.axis_index("code")
    barrier = pltpu.get_barrier_semaphore()
    for k in range(1, n_code):
        pl.semaphore_signal(barrier, inc=1, device_id=(d, (o + k) % n_code), device_id_type=MESH)
    for k in range(n_code):
        peer = (o + k) % n_code
        block = book_ref[ids_ref[d * n_code + peer]]
        if k == 0:
            out_ref[o] = block
        else:
            stage[k] = block
    pl.semaphore_wait(barrier, n_code - 1)
    copies = []
    for k in range(1, n_code):
        copy = pltpu.make_async_remote_copy(
            src_ref=stage.at[k],
            dst_ref=out_ref.at[o],
            send_sem=send_sem.at[k],
            recv_sem=recv_sem.at[k],
            device_id=(d, (o + k) % n_code),
            device_id_type=MESH,
        )
        copy.start()
        copies.append(copy)
    for copy in copies:
        copy.wait()


def gather_kernel(
    n_dp, n_code, sums_ref, out_ref, a_send, a_recv, y_send, y_recv, c_send, c_recv, own_sem
):
    d = lax.axis_index("dp")
    o = lax.axis_index("code")
    n_y = n_dp // 2
    y = d // 2
    core = d % 2
    mate = y * 2 + 1 - core
    barrier = pltpu.get_barrier_semaphore()
    for k in range(1, n_code):
        pl.semaphore_signal(barrier, inc=1, device_id=(d, (o + k) % n_code), device_id_type=MESH)
    for j in range(1, n_y):
        pl.semaphore_signal(
            barrier, inc=1, device_id=((y + j) % n_y * 2 + core, o), device_id_type=MESH
        )
    pl.semaphore_signal(barrier, inc=1, device_id=(mate, o), device_id_type=MESH)
    own = pltpu.make_async_copy(sums_ref.at[o], out_ref.at[d * n_code + o], own_sem)
    own.start()
    pl.semaphore_wait(barrier, n_code - 1 + n_y - 1 + 1)

    waits = []
    across = []
    for k in range(1, n_code):
        copy = pltpu.make_async_remote_copy(
            src_ref=sums_ref.at[(o + k) % n_code],
            dst_ref=out_ref.at[d * n_code + o],
            send_sem=a_send.at[k],
            recv_sem=a_recv.at[k],
            device_id=(d, (o + k) % n_code),
            device_id_type=MESH,
        )
        copy.start()
        across.append(copy)
        waits.append(copy.wait_send)

    def to_y(k, j):
        row = d * n_code + (o + n_code - k) % n_code
        return pltpu.make_async_remote_copy(
            src_ref=out_ref.at[row],
            dst_ref=out_ref.at[row],
            send_sem=y_send.at[j, k],
            recv_sem=y_recv.at[j, k],
            device_id=((y + j) % n_y * 2 + core, o),
            device_id_type=MESH,
        )

    def to_mate(k, j):
        row = ((y + n_y - j) % n_y * 2 + core) * n_code + (o + n_code - k) % n_code
        return pltpu.make_async_remote_copy(
            src_ref=out_ref.at[row],
            dst_ref=out_ref.at[row],
            send_sem=c_send.at[j, k],
            recv_sem=c_recv.at[j, k],
            device_id=(mate, o),
            device_id_type=MESH,
        )

    y_copies = {}
    for k in range(n_code):
        if k == 0:
            own.wait()
        else:
            across[k - 1].wait_recv()
        for j in range(1, n_y):
            copy = to_y(k, j)
            copy.start()
            y_copies[j, k] = copy
            waits.append(copy.wait_send)
        copy = to_mate(k, 0)
        copy.start()
        waits.append(copy.wait_send)
        waits.append(copy.wait_recv)
    for k in range(n_code):
        for j in range(1, n_y):
            y_copies[j, k].wait_recv()
            copy = to_mate(k, j)
            copy.start()
            waits.append(copy.wait_send)
            waits.append(copy.wait_recv)
    for wait in waits:
        wait()


def update_kernel(n, own_blocks, ids_ref, con_ref, book_ref, out_ref, sums, mass):
    sums[...] = book_ref[...]
    mass[...] = jnp.ones_like(mass)

    def add(j, c):
        b = ids_ref[j]
        sums[b] += con_ref[j, :CBLK]
        mass[b] += con_ref[j, CBLK:]
        return c

    lax.fori_loop(0, n, add, 0)

    def finish(b, c):
        for h in range(2):
            inv = 1.0 / mass[b, pl.ds(h, 1), :]
            column = jnp.transpose(jnp.broadcast_to(inv, (128, 128)))
            rows = pl.ds(h * 128, 128)
            out_ref[b, rows, :] = sums[b, rows, :] * column
        return c

    lax.fori_loop(0, own_blocks, finish, 0)


def assign_kernel(
    n_slots, key_blocks, block, feature,
    slots_ref, counts_ref, fetched_ref, keys_ref,
    sums_ref, logsum_ref,
    words, kst, kext, scores, acc, top,
):
    inv_scale = 1.0 / math.sqrt(feature)
    log2e = math.log2(math.e)
    lane = lax.broadcasted_iota(jnp.int32, (CBLK, 128), 1)

    def split(value):
        hi = value.astype(jnp.bfloat16)
        rest = value - hi.astype(jnp.float32)
        mid = rest.astype(jnp.bfloat16)
        lo = (rest - mid.astype(jnp.float32)).astype(jnp.bfloat16)
        return hi, mid, lo

    def prepare(s, c):
        value = fetched_ref[s]
        hi, mid, lo = split(value)
        words[s, :, 0:128] = hi
        words[s, :, 128:256] = mid
        words[s, :, 256:384] = lo
        half = -0.5 * jnp.sum(value * value, axis=1, keepdims=True)
        n_hi, n_mid, n_lo = [t.astype(jnp.float32) for t in split(half)]
        extra = jnp.where(
            lane == 0, n_hi, jnp.where(lane == 1, n_mid, jnp.where(lane == 2, n_lo, 0.0))
        )
        words[s, :, 384:512] = extra.astype(jnp.bfloat16)
        acc[s] = jnp.zeros((CBLK, 256), jnp.float32)
        return c

    lax.fori_loop(0, n_slots, prepare, 0)
    kst[384:512, :] = jnp.ones((128, block), jnp.bfloat16)
    kext[:, 128:256] = jnp.ones((block, 128), jnp.bfloat16)

    def key_block(kb, c):
        keys = keys_ref[pl.ds(pl.multiple_of(kb * block, block), block), :]
        kext[:, 0:128] = keys
        turned = jnp.transpose(keys)
        kst[0:128, :] = turned
        kst[128:256, :] = turned
        kst[256:384, :] = turned
        count = counts_ref[kb]
        top[...] = jnp.full((8, block), -3e38, jnp.float32)

        def score(l, c2):
            s = jnp.dot(words[slots_ref[kb, l]], kst[...], preferred_element_type=jnp.float32)
            scores[l] = s
            top[...] = jnp.maximum(top[...], jnp.max(s.reshape(CBLK // 8, 8, block), axis=0))
            return c2

        lax.fori_loop(0, count, score, 0)
        peak = jnp.max(top[...], axis=0, keepdims=True)

        def expo(l, total):
            e = jnp.exp2((scores[l] - peak) * (inv_scale * log2e))
            scores[l] = e
            return total + jnp.sum(e.reshape(CBLK // 8, 8, block), axis=0)

        total = lax.fori_loop(0, count, expo, jnp.zeros((8, block), jnp.float32))
        total = jnp.sum(total, axis=0, keepdims=True)
        logsum_ref[kb] = peak * inv_scale + jnp.log(total)
        inv = 1.0 / total

        def spread(l, c2):
            p = (scores[l] * inv).astype(jnp.bfloat16)
            slot = slots_ref[kb, l]
            acc[slot] += jnp.dot(p, kext[...], preferred_element_type=jnp.float32)
            return c2

        lax.fori_loop(0, count, spread, 0)
        return c

    lax.fori_loop(0, key_blocks, key_block, 0)

    def write(s, c):
        sums_ref[s, :CBLK, :] = acc[s, :, 0:128]
        for h in range(2):
            turned = jnp.transpose(acc[s, pl.ds(h * 128, 128), pl.ds(128, 128)])
            sums_ref[s, pl.ds(CBLK + h, 1), :] = turned[0:1, :]
        sums_ref[s, CBLK + 2 :, :] = jnp.zeros((MROWS - 2, 128), jnp.float32)
        return c

    lax.fori_loop(0, n_slots, write, 0)


def on_device(cached_keys, codebook, block_lists, counts):
    n_dp = lax.axis_size("dp")
    n_code = lax.axis_size("code")
    n = n_dp * n_code
    own_rows, feature = codebook.shape
    own_blocks = own_rows // CBLK
    key_blocks = block_lists.shape[0]
    block = cached_keys.shape[0] // key_blocks
    f32 = jnp.float32
    dma = pltpu.SemaphoreType.DMA

    slots = block_lists // own_blocks
    local = block_lists % own_blocks
    wanted = jnp.max(
        jnp.where(
            slots.reshape(-1)[:, None] == jnp.arange(128)[None, :], local.reshape(-1)[:, None], 0
        ),
        axis=0,
    )
    everyone = pl.pallas_call(
        functools.partial(ids_kernel, n_dp, n_code),
        out_shape=jax.ShapeDtypeStruct((n, 8, 128), jnp.int32),
        in_specs=[VM],
        out_specs=VM,
        scratch_shapes=[dma((n,)), dma((n,))],
        compiler_params=pltpu.CompilerParams(collective_id=0, has_side_effects=True),
    )(jnp.broadcast_to(wanted[None, :], (8, 128)).astype(jnp.int32))
    ids = lax.dynamic_index_in_dim(everyone[:, 0, :], lax.axis_index("code"), 1, keepdims=False)

    current = codebook.reshape(own_blocks, CBLK, feature)
    logsum = None
    for sweep in range(ITERS):
        fetched = pl.pallas_call(
            functools.partial(fetch_kernel, n_code),
            out_shape=jax.ShapeDtypeStruct((n_code, CBLK, feature), f32),
            in_specs=[SM, VM],
            out_specs=VM,
            scratch_shapes=[
                pltpu.VMEM((n_code, CBLK, feature), f32), dma((n_code,)), dma((n_code,))
            ],
            compiler_params=pltpu.CompilerParams(
                collective_id=1 + 2 * sweep, has_side_effects=True, vmem_limit_bytes=VLIMIT
            ),
        )(ids, current)
        sums, logsum = pl.pallas_call(
            functools.partial(assign_kernel, n_code, key_blocks, block, feature),
            out_shape=(
                jax.ShapeDtypeStruct((n_code, CBLK + MROWS, feature), f32),
                jax.ShapeDtypeStruct((key_blocks, 1, block), f32),
            ),
            in_specs=[SM, SM, VM, VM],
            out_specs=(VM, VM),
            scratch_shapes=[
                pltpu.VMEM((n_code, CBLK, 512), jnp.bfloat16),
                pltpu.VMEM((512, block), jnp.bfloat16),
                pltpu.VMEM((block, 256), jnp.bfloat16),
                pltpu.VMEM((LIST_MAX, CBLK, block), f32),
                pltpu.VMEM((n_code, CBLK, 256), f32),
                pltpu.VMEM((8, block), f32),
            ],
            compiler_params=pltpu.CompilerParams(vmem_limit_bytes=VLIMIT),
        )(slots, counts, fetched, cached_keys)
        n_y = n_dp // 2
        gathered = pl.pallas_call(
            functools.partial(gather_kernel, n_dp, n_code),
            out_shape=jax.ShapeDtypeStruct((n, CBLK + MROWS, feature), f32),
            in_specs=[VM],
            out_specs=VM,
            scratch_shapes=[
                dma((n_code,)), dma((n_code,)),
                dma((n_y, n_code)), dma((n_y, n_code)),
                dma((n_y, n_code)), dma((n_y, n_code)),
                dma,
            ],
            compiler_params=pltpu.CompilerParams(
                collective_id=2 + 2 * sweep, has_side_effects=True, vmem_limit_bytes=VLIMIT
            ),
        )(sums)
        current = pl.pallas_call(
            functools.partial(update_kernel, n, own_blocks),
            out_shape=jax.ShapeDtypeStruct((own_blocks, CBLK, feature), f32),
            in_specs=[SM, VM, VM],
            out_specs=VM,
            scratch_shapes=[
                pltpu.VMEM((own_blocks, CBLK, feature), f32),
                pltpu.VMEM((own_blocks, MROWS, feature), f32),
            ],
            compiler_params=pltpu.CompilerParams(vmem_limit_bytes=VLIMIT),
        )(ids, gathered, current)
    return (current.reshape(own_rows, feature), logsum.reshape(-1))


def solution(mesh):
    in_specs = (
        P(("dp", "code"), None),
        P("code", None),
        P(("dp", "code"), None),
        P(("dp", "code")),
    )
    out_specs = (P("code", None), P(("dp", "code")))
    return jax.shard_map(
        on_device, mesh=mesh, in_specs=in_specs, out_specs=out_specs, check_vma=False
    )
```

```python
import functools
import math

import jax
import jax.numpy as jnp
from jax import lax
from jax.experimental import pallas as pl
from jax.experimental.pallas import tpu as pltpu
from jax.sharding import PartitionSpec as P

CBLK = 256
LIST_MAX = 6
ITERS = 2
MROWS = 8
MESH = pl.DeviceIdType.MESH
VLIMIT = 60 * 1024 * 1024
HELD_BYTES = 16 * 1024 * 1024

VM = pl.BlockSpec(memory_space=pltpu.VMEM)
SM = pl.BlockSpec(memory_space=pltpu.SMEM)
ANY = pl.BlockSpec(memory_space=pl.ANY)


def flip(value, bits):
    out = value
    bit = 1
    while bit <= bits:
        if bits & bit:
            out = out + bit * (1 - 2 * (value // bit % 2))
        bit *= 2
    return out


def remote(src, dst, send, recv, dp, code):
    return pltpu.make_async_remote_copy(
        src_ref=src, dst_ref=dst, send_sem=send, recv_sem=recv,
        device_id=(dp, code), device_id_type=MESH,
    )


def fetch_kernel(
    n_code, want_ref, book_hbm, out_ref, served_ref, asked_ref,
    book, ids, id_send, id_recv, send_sem, recv_sem, book_sem, own_sem, smem_sem,
):
    d = lax.axis_index("dp")
    o = lax.axis_index("code")
    barrier = pltpu.get_barrier_semaphore()
    for k in range(1, n_code):
        pl.semaphore_signal(barrier, inc=1, device_id=(d, flip(o, k)), device_id_type=MESH)
    load = pltpu.make_async_copy(book_hbm, book, book_sem)
    load.start()
    own = pltpu.make_async_copy(want_ref.at[o], asked_ref.at[o], own_sem)
    own.start()
    pl.semaphore_wait(barrier, n_code - 1)
    asks = []
    for k in range(1, n_code):
        peer = flip(o, k)
        copy = remote(
            want_ref.at[peer], asked_ref.at[o], id_send.at[k], id_recv.at[k], d, peer
        )
        copy.start()
        asks.append(copy)
    load.wait()
    copies = []
    for k in range(1, n_code):
        peer = flip(o, k)
        asks[k - 1].wait_recv()
        move = pltpu.make_async_copy(asked_ref.at[peer], ids.at[k], smem_sem.at[k])
        move.start()
        move.wait()
        served_ref[peer] = book[ids[k, 0, 0]]
        copy = remote(
            served_ref.at[peer], out_ref.at[o], send_sem.at[k], recv_sem.at[k], d, peer
        )
        copy.start()
        copies.append(copy)
    own.wait()
    move = pltpu.make_async_copy(asked_ref.at[o], ids.at[0], smem_sem.at[0])
    move.start()
    move.wait()
    block = book[ids[0, 0, 0]]
    served_ref[o] = block
    out_ref[o] = block
    for ask in asks:
        ask.wait_send()
    for copy in copies:
        copy.wait()


def exchange_kernel(n_dp, n_code, reply, *refs):
    if reply:
        (sums_ref, served_ref, asked_ref, con_ref, back_ref, acc, stage,
         a_send, a_recv, y_send, y_recv, c_send, c_recv, own_sem, b_send, b_recv) = refs
    else:
        (sums_ref, con_ref,
         a_send, a_recv, y_send, y_recv, c_send, c_recv, own_sem) = refs
    d = lax.axis_index("dp")
    o = lax.axis_index("code")
    n_y = n_dp // 2
    y = d // 2
    core = d % 2
    mate = y * 2 + 1 - core
    barrier = pltpu.get_barrier_semaphore()
    for k in range(1, n_code):
        pl.semaphore_signal(barrier, inc=1, device_id=(d, flip(o, k)), device_id_type=MESH)
    for j in range(1, n_y):
        pl.semaphore_signal(
            barrier, inc=1, device_id=((y + j) % n_y * 2 + core, o), device_id_type=MESH
        )
    pl.semaphore_signal(barrier, inc=1, device_id=(mate, o), device_id_type=MESH)
    own = pltpu.make_async_copy(sums_ref.at[o], con_ref.at[d * n_code + o], own_sem)
    own.start()
    pl.semaphore_wait(barrier, n_code - 1 + n_y - 1 + 1)

    sends = []
    across = []
    for k in range(1, n_code):
        peer = flip(o, k)
        copy = remote(
            sums_ref.at[peer], con_ref.at[d * n_code + o], a_send.at[k], a_recv.at[k], d, peer
        )
        copy.start()
        across.append(copy)
        sends.append(copy)

    def to_y(k, j):
        row = d * n_code + flip(o, k)
        return remote(
            con_ref.at[row], con_ref.at[row], y_send.at[j, k], y_recv.at[j, k],
            (y + j) % n_y * 2 + core, o,
        )

    def held(k, j):
        return ((y + n_y - j) % n_y * 2 + core) * n_code + flip(o, k)

    def to_mate(k, j):
        row = held(k, j)
        return remote(
            con_ref.at[row], con_ref.at[row], c_send.at[j, k], c_recv.at[j, k], mate, o
        )

    if reply:
        acc[...] = jnp.zeros_like(acc)

    def absorb(row):
        if not reply:
            return
        here = con_ref[row, pl.ds(CBLK + 2, 1), :]

        def one(i, c):
            same = (asked_ref[i, pl.ds(0, 1), :].astype(jnp.float32) == here).astype(jnp.float32)
            acc[i] += con_ref[row] * same
            return c

        lax.fori_loop(0, n_code, one, 0)

    y_copies = {}
    mates = {}
    for k in range(n_code):
        if k == 0:
            own.wait()
        else:
            across[k - 1].wait_recv()
        for j in range(1, n_y):
            copy = to_y(k, j)
            copy.start()
            y_copies[j, k] = copy
            sends.append(copy)
        copy = to_mate(k, 0)
        copy.start()
        mates[0, k] = copy
        sends.append(copy)
        absorb(held(k, 0))
    for k in range(n_code):
        for j in range(1, n_y):
            y_copies[j, k].wait_recv()
            copy = to_mate(k, j)
            copy.start()
            mates[j, k] = copy
            sends.append(copy)
            absorb(held(k, j))
    for k in range(n_code):
        for j in range(n_y):
            mates[j, k].wait_recv()
            absorb(held(k, j) + (1 - 2 * core) * n_code)
    if reply:
        backs = []
        for k in range(n_code):
            peer = flip(o, k)
            for h in range(2):
                inv = 1.0 / (acc[peer, pl.ds(CBLK + h, 1), :] + 1.0)
                column = jnp.transpose(jnp.broadcast_to(inv, (128, 128)))
                rows = pl.ds(h * 128, 128)
                fresh = (acc[peer, rows, :] + served_ref[peer, rows, :]) * column
                if k == 0:
                    back_ref[o, rows, :] = fresh
                else:
                    stage[k, rows, :] = fresh
        for k in range(n_code - 1, 0, -1):
            copy = remote(
                stage.at[k], back_ref.at[o], b_send.at[k], b_recv.at[k], d, flip(o, k)
            )
            copy.start()
            backs.append(copy)
        for copy in backs:
            copy.wait()
    for copy in sends:
        copy.wait_send()


def finish_kernel(
    n, own_blocks, sweeps, *refs
):
    con_hbm = refs[:sweeps]
    book_hbm, out_hbm = refs[sweeps : sweeps + 2]
    con, total, ids, con_sem, book_sem, out_sem = refs[sweeps + 2 :]
    book = pltpu.make_async_copy(book_hbm, total.at[:, pl.ds(0, CBLK), :], book_sem)
    book.start()
    half = n // 2

    def load(t, h):
        rows = pl.ds(h * half, half)
        return pltpu.make_async_copy(con_hbm[t].at[rows], con.at[rows], con_sem.at[h])

    load(0, 0).start()
    load(0, 1).start()
    book.wait()
    for t in range(sweeps):
        total[:, CBLK:, :] = jnp.ones((own_blocks, MROWS, 128), jnp.float32)
        for h in range(2):
            load(t, h).wait()

            def add(j, c):
                if t == 0:
                    ids[j] = con_ids(con, j)
                b = ids[j]
                total[b] += con[j]
                return c

            lax.fori_loop(h * half, (h + 1) * half, add, 0)
            if t + 1 < sweeps:
                load(t + 1, h).start()

        def scale(b, c):
            for h in range(2):
                inv = 1.0 / total[b, pl.ds(CBLK + h, 1), :]
                column = jnp.transpose(jnp.broadcast_to(inv, (128, 128)))
                rows = pl.ds(h * 128, 128)
                total[b, rows, :] = total[b, rows, :] * column
            return c

        lax.fori_loop(0, own_blocks, scale, 0)
    out = pltpu.make_async_copy(total.at[:, pl.ds(0, CBLK), :], out_hbm, out_sem)
    out.start()
    out.wait()


def con_ids(con, j):
    return jnp.max(con[j, pl.ds(CBLK + 2, 1), :]).astype(jnp.int32)


def assign_kernel(
    n_slots, key_blocks, block, feature,
    slots_ref, counts_ref, fetched_ref, keys_ref, want_ref,
    sums_ref, logsum_ref,
    words, norms, kst, kext, scores, acc, top,
):
    inv_scale = 1.0 / math.sqrt(feature)
    log2e = math.log2(math.e)

    def prepare(s, c):
        value = fetched_ref[s]
        hi = value.astype(jnp.bfloat16)
        words[s, :, 0:128] = hi
        words[s, :, 128:256] = (value - hi.astype(jnp.float32)).astype(jnp.bfloat16)
        half = 0.5 * jnp.sum(value * value, axis=1, keepdims=True)
        norms[s] = jnp.broadcast_to(half, (CBLK, 128))
        acc[s] = jnp.zeros((CBLK, 256), jnp.float32)
        return c

    lax.fori_loop(0, n_slots, prepare, 0)
    kext[:, 128:256] = jnp.ones((block, 128), jnp.bfloat16)

    def key_block(kb, c):
        keys = keys_ref[pl.ds(pl.multiple_of(kb * block, block), block), :]
        kext[:, 0:128] = keys
        turned = jnp.transpose(keys)
        kst[0:128, :] = turned
        kst[128:256, :] = turned
        count = counts_ref[kb]
        top[...] = jnp.full((8, block), -3e38, jnp.float32)

        def score(l, c2):
            slot = slots_ref[kb, l]
            s = jnp.dot(words[slot], kst[...], preferred_element_type=jnp.float32)
            s = s - jnp.tile(norms[slot], (1, block // 128))
            scores[l] = s
            top[...] = jnp.maximum(top[...], jnp.max(s.reshape(CBLK // 8, 8, block), axis=0))
            return c2

        lax.fori_loop(0, count, score, 0)
        peak = jnp.max(top[...], axis=0, keepdims=True)

        def expo(l, total):
            e = jnp.exp2((scores[l] - peak) * (inv_scale * log2e))
            scores[l] = e
            return total + jnp.sum(e.reshape(CBLK // 8, 8, block), axis=0)

        total = lax.fori_loop(0, count, expo, jnp.zeros((8, block), jnp.float32))
        total = jnp.sum(total, axis=0, keepdims=True)
        logsum_ref[kb] = peak * inv_scale + jnp.log(total)
        inv = 1.0 / total

        def spread(l, c2):
            p = (scores[l] * inv).astype(jnp.bfloat16)
            slot = slots_ref[kb, l]
            acc[slot] += jnp.dot(p, kext[...], preferred_element_type=jnp.float32)
            return c2

        lax.fori_loop(0, count, spread, 0)
        return c

    lax.fori_loop(0, key_blocks, key_block, 0)

    def write(s, c):
        sums_ref[s, :CBLK, :] = acc[s, :, 0:128]
        for h in range(2):
            turned = jnp.transpose(acc[s, pl.ds(h * 128, 128), pl.ds(128, 128)])
            sums_ref[s, pl.ds(CBLK + h, 1), :] = turned[0:1, :]
        sums_ref[s, CBLK + 2 :, :] = want_ref[s, 2:, :].astype(jnp.float32)
        return c

    lax.fori_loop(0, n_slots, write, 0)


def on_device(cached_keys, codebook, block_lists, counts):
    n_dp = lax.axis_size("dp")
    n_code = lax.axis_size("code")
    n = n_dp * n_code
    own_rows, feature = codebook.shape
    own_blocks = own_rows // CBLK
    key_blocks = block_lists.shape[0]
    block = cached_keys.shape[0] // key_blocks
    f32 = jnp.float32
    dma = pltpu.SemaphoreType.DMA

    slots = block_lists // own_blocks
    local = block_lists % own_blocks
    wanted = jnp.max(
        jnp.where(
            slots.reshape(-1)[:, None] == jnp.arange(128)[None, :], local.reshape(-1)[:, None], 0
        ),
        axis=0,
    )
    want = jnp.broadcast_to(wanted[:n_code, None, None], (n_code, 8, 128)).astype(jnp.int32)
    blocks = jax.ShapeDtypeStruct((n_code, CBLK, feature), f32)
    sums_shape = jax.ShapeDtypeStruct((n_code, CBLK + MROWS, feature), f32)
    con_shape = jax.ShapeDtypeStruct((n, CBLK + MROWS, feature), f32)
    n_y = n_dp // 2

    def params(**kw):
        return pltpu.CompilerParams(vmem_limit_bytes=VLIMIT, **kw)

    book = codebook.reshape(own_blocks, CBLK, feature)
    fetched, served, asked = pl.pallas_call(
        functools.partial(fetch_kernel, n_code),
        out_shape=(blocks, blocks, jax.ShapeDtypeStruct((n_code, 8, 128), jnp.int32)),
        in_specs=[VM, ANY],
        out_specs=(VM, VM, VM),
        scratch_shapes=[
            pltpu.VMEM((own_blocks, CBLK, feature), f32),
            pltpu.SMEM((n_code, 8, 128), jnp.int32),
            dma((n_code,)), dma((n_code,)), dma((n_code,)), dma((n_code,)),
            dma, dma, dma((n_code,)),
        ],
        compiler_params=params(collective_id=0, has_side_effects=True),
    )(want, book)
    logsum = None
    gathered = []
    current = book
    joint = ITERS * n * (CBLK + MROWS) * feature * 4 <= HELD_BYTES

    def finish(parts, held):
        return pl.pallas_call(
            functools.partial(finish_kernel, n, own_blocks, len(parts)),
            out_shape=jax.ShapeDtypeStruct((own_blocks, CBLK, feature), f32),
            in_specs=[ANY] * (len(parts) + 1),
            out_specs=ANY,
            scratch_shapes=[
                pltpu.VMEM(con_shape.shape, f32),
                pltpu.VMEM((own_blocks, CBLK + MROWS, feature), f32),
                pltpu.SMEM((n,), jnp.int32),
                dma((2,)), dma, dma,
            ],
            compiler_params=params(),
        )(*parts, held)

    for sweep in range(ITERS):
        sums, logsum = pl.pallas_call(
            functools.partial(assign_kernel, n_code, key_blocks, block, feature),
            out_shape=(sums_shape, jax.ShapeDtypeStruct((key_blocks, 1, block), f32)),
            in_specs=[SM, SM, VM, VM, VM],
            out_specs=(VM, VM),
            scratch_shapes=[
                pltpu.VMEM((n_code, CBLK, 256), jnp.bfloat16),
                pltpu.VMEM((n_code, CBLK, 128), f32),
                pltpu.VMEM((256, block), jnp.bfloat16),
                pltpu.VMEM((block, 256), jnp.bfloat16),
                pltpu.VMEM((LIST_MAX, CBLK, block), f32),
                pltpu.VMEM((n_code, CBLK, 256), f32),
                pltpu.VMEM((8, block), f32),
            ],
            compiler_params=params(),
        )(slots, counts, fetched, cached_keys, want)
        reply = sweep + 1 < ITERS
        sems = [
            dma((n_code,)), dma((n_code,)),
            dma((n_y, n_code)), dma((n_y, n_code)),
            dma((n_y, n_code)), dma((n_y, n_code)),
            dma,
        ]
        if reply:
            con, fetched = pl.pallas_call(
                functools.partial(exchange_kernel, n_dp, n_code, True),
                out_shape=(con_shape, blocks),
                in_specs=[VM, VM, VM],
                out_specs=(VM, VM),
                scratch_shapes=[
                    pltpu.VMEM(sums_shape.shape, f32), pltpu.VMEM(blocks.shape, f32)
                ] + sems + [dma((n_code,)), dma((n_code,))],
                compiler_params=params(collective_id=1 + sweep, has_side_effects=True),
            )(sums, served, asked)
        else:
            con = pl.pallas_call(
                functools.partial(exchange_kernel, n_dp, n_code, False),
                out_shape=con_shape,
                in_specs=[VM],
                out_specs=VM,
                scratch_shapes=sems,
                compiler_params=params(collective_id=1 + sweep, has_side_effects=True),
            )(sums)
        gathered.append(con)
        if not joint:
            current = finish(gathered, current)
            gathered = []
            if reply:
                current, fetched = lax.optimization_barrier((current, fetched))
    if gathered:
        current = finish(gathered, current)
    return (current.reshape(own_rows, feature), logsum.reshape(-1))


def solution(mesh):
    in_specs = (
        P(("dp", "code"), None),
        P("code", None),
        P(("dp", "code"), None),
        P(("dp", "code")),
    )
    out_specs = (P("code", None), P(("dp", "code")))
    return jax.shard_map(
        on_device, mesh=mesh, in_specs=in_specs, out_specs=out_specs, check_vma=False
    )
```

```python
import functools
import math

import jax
import jax.numpy as jnp
from jax import lax
from jax.experimental import pallas as pl
from jax.experimental.pallas import tpu as pltpu
from jax.sharding import PartitionSpec as P

CBLK = 256
LIST_MAX = 6
ITERS = 2
MROWS = 8
MESH = pl.DeviceIdType.MESH
VLIMIT = 60 * 1024 * 1024
HELD_BYTES = 16 * 1024 * 1024

VM = pl.BlockSpec(memory_space=pltpu.VMEM)
SM = pl.BlockSpec(memory_space=pltpu.SMEM)
ANY = pl.BlockSpec(memory_space=pl.ANY)


def flip(value, bits):
    out = value
    bit = 1
    while bit <= bits:
        if bits & bit:
            out = out + bit * (1 - 2 * (value // bit % 2))
        bit *= 2
    return out


def remote(src, dst, send, recv, dp, code):
    return pltpu.make_async_remote_copy(
        src_ref=src, dst_ref=dst, send_sem=send, recv_sem=recv,
        device_id=(dp, code), device_id_type=MESH,
    )


def fetch_kernel(
    n_code, want_ref, book_hbm, out_ref, served_ref, asked_ref,
    book, ids, id_send, id_recv, send_sem, recv_sem, book_sem, own_sem, smem_sem,
):
    d = lax.axis_index("dp")
    o = lax.axis_index("code")
    barrier = pltpu.get_barrier_semaphore()
    for k in range(1, n_code):
        pl.semaphore_signal(barrier, inc=1, device_id=(d, flip(o, k)), device_id_type=MESH)
    load = pltpu.make_async_copy(book_hbm, book, book_sem)
    load.start()
    own = pltpu.make_async_copy(want_ref.at[o], asked_ref.at[o], own_sem)
    own.start()
    pl.semaphore_wait(barrier, n_code - 1)
    asks = []
    for k in range(1, n_code):
        peer = flip(o, k)
        copy = remote(
            want_ref.at[peer], asked_ref.at[o], id_send.at[k], id_recv.at[k], d, peer
        )
        copy.start()
        asks.append(copy)
    load.wait()
    copies = []
    for k in range(1, n_code):
        peer = flip(o, k)
        asks[k - 1].wait_recv()
        move = pltpu.make_async_copy(asked_ref.at[peer], ids.at[k], smem_sem.at[k])
        move.start()
        move.wait()
        served_ref[peer] = book[ids[k, 0, 0]]
        copy = remote(
            served_ref.at[peer], out_ref.at[o], send_sem.at[k], recv_sem.at[k], d, peer
        )
        copy.start()
        copies.append(copy)
    own.wait()
    move = pltpu.make_async_copy(asked_ref.at[o], ids.at[0], smem_sem.at[0])
    move.start()
    move.wait()
    block = book[ids[0, 0, 0]]
    served_ref[o] = block
    out_ref[o] = block
    for ask in asks:
        ask.wait_send()
    for copy in copies:
        copy.wait()


def exchange_kernel(n_dp, n_code, reply, *refs):
    if reply:
        (sums_ref, served_ref, asked_ref, con_ref, back_ref, acc, stage,
         a_send, a_recv, y_send, y_recv, c_send, c_recv, own_sem, b_send, b_recv) = refs
    else:
        (sums_ref, con_ref,
         a_send, a_recv, y_send, y_recv, c_send, c_recv, own_sem) = refs
    d = lax.axis_index("dp")
    o = lax.axis_index("code")
    n_y = n_dp // 2
    y = d // 2
    core = d % 2
    mate = y * 2 + 1 - core
    barrier = pltpu.get_barrier_semaphore()
    for k in range(1, n_code):
        pl.semaphore_signal(barrier, inc=1, device_id=(d, flip(o, k)), device_id_type=MESH)
    for j in range(1, n_y):
        pl.semaphore_signal(
            barrier, inc=1, device_id=((y + j) % n_y * 2 + core, o), device_id_type=MESH
        )
    pl.semaphore_signal(barrier, inc=1, device_id=(mate, o), device_id_type=MESH)
    own = pltpu.make_async_copy(sums_ref.at[o], con_ref.at[d * n_code + o], own_sem)
    own.start()
    pl.semaphore_wait(barrier, n_code - 1 + n_y - 1 + 1)

    sends = []
    across = []
    for k in range(1, n_code):
        peer = flip(o, k)
        copy = remote(
            sums_ref.at[peer], con_ref.at[d * n_code + o], a_send.at[k], a_recv.at[k], d, peer
        )
        copy.start()
        across.append(copy)
        sends.append(copy)

    def to_y(k, j):
        row = d * n_code + flip(o, k)
        return remote(
            con_ref.at[row], con_ref.at[row], y_send.at[j, k], y_recv.at[j, k],
            (y + j) % n_y * 2 + core, o,
        )

    def held(k, j):
        return ((y + n_y - j) % n_y * 2 + core) * n_code + flip(o, k)

    def to_mate(k, j):
        row = held(k, j)
        return remote(
            con_ref.at[row], con_ref.at[row], c_send.at[j, k], c_recv.at[j, k], mate, o
        )

    if reply:
        acc[...] = jnp.zeros_like(acc)

    def absorb(row):
        if not reply:
            return
        here = con_ref[row, pl.ds(CBLK + 2, 1), :]

        def one(i, c):
            same = (asked_ref[i, pl.ds(0, 1), :].astype(jnp.float32) == here).astype(jnp.float32)
            acc[i] += con_ref[row] * same
            return c

        lax.fori_loop(0, n_code, one, 0)

    y_copies = {}
    mates = {}
    for k in range(n_code):
        if k == 0:
            own.wait()
        else:
            across[k - 1].wait_recv()
        for j in range(1, n_y):
            copy = to_y(k, j)
            copy.start()
            y_copies[j, k] = copy
            sends.append(copy)
        copy = to_mate(k, 0)
        copy.start()
        mates[0, k] = copy
        sends.append(copy)
        absorb(held(k, 0))
    for k in range(n_code):
        for j in range(1, n_y):
            y_copies[j, k].wait_recv()
            copy = to_mate(k, j)
            copy.start()
            mates[j, k] = copy
            sends.append(copy)
            absorb(held(k, j))
        mates[0, k].wait_recv()
        absorb(held(k, 0) + (1 - 2 * core) * n_code)
    for k in range(n_code):
        for j in range(1, n_y):
            mates[j, k].wait_recv()
            absorb(held(k, j) + (1 - 2 * core) * n_code)
    if reply:
        backs = []
        for k in range(n_code):
            peer = flip(o, k)
            for h in range(2):
                inv = 1.0 / (acc[peer, pl.ds(CBLK + h, 1), :] + 1.0)
                column = jnp.transpose(jnp.broadcast_to(inv, (128, 128)))
                rows = pl.ds(h * 128, 128)
                fresh = (acc[peer, rows, :] + served_ref[peer, rows, :]) * column
                if k == 0:
                    back_ref[o, rows, :] = fresh
                else:
                    stage[k, rows, :] = fresh
        for k in range(n_code - 1, 0, -1):
            copy = remote(
                stage.at[k], back_ref.at[o], b_send.at[k], b_recv.at[k], d, flip(o, k)
            )
            copy.start()
            backs.append(copy)
        for copy in backs:
            copy.wait()
    for copy in sends:
        copy.wait_send()


def finish_kernel(n, own_blocks, sweeps, *refs):
    con_hbm = refs[:sweeps]
    book_hbm, out_hbm = refs[sweeps : sweeps + 2]
    con, total, mass, ids, con_sem, book_sem, out_sem = refs[sweeps + 2 :]
    book = pltpu.make_async_copy(book_hbm, total, book_sem)
    book.start()
    half = n // 2

    def load(t, h):
        rows = pl.ds(h * half, half)
        return pltpu.make_async_copy(con_hbm[t].at[rows], con.at[rows], con_sem.at[h])

    load(0, 0).start()
    load(0, 1).start()
    outs = []
    for t in range(sweeps):
        mass[...] = jnp.ones_like(mass)
        for h in range(2):
            load(t, h).wait()
            if t == 0:

                def name(j, c):
                    for u in range(4):
                        i = j * 4 + u
                        ids[i] = jnp.max(con[i, pl.ds(CBLK + 2, 1), :]).astype(jnp.int32)
                    return c

                lax.fori_loop(h * half // 4, (h + 1) * half // 4, name, 0)
                if h == 0:
                    book.wait()

            def add(j, c):
                b = ids[j]
                total[b] += con[j, :CBLK, :]
                for g in range(2):
                    row = pl.ds(g * (mass.shape[0] // 2) + b, 1)
                    mass[row, :] += con[j, pl.ds(CBLK + g, 1), :]
                return c

            lax.fori_loop(h * half, (h + 1) * half, add, 0)
            if t + 1 < sweeps:
                load(t + 1, h).start()
        columns = jnp.transpose(1.0 / mass[...])
        for b in range(own_blocks):
            for g in range(2):
                lane = g * (mass.shape[0] // 2) + b
                total[b, g * 128 : (g + 1) * 128, :] = (
                    total[b, g * 128 : (g + 1) * 128, :] * columns[:, lane : lane + 1]
                )
            if t + 1 == sweeps:
                out = pltpu.make_async_copy(total.at[b], out_hbm.at[b], out_sem.at[b])
                out.start()
                outs.append(out)
    for out in outs:
        out.wait()


def assign_kernel(
    n_slots, key_blocks, block, feature,
    slots_ref, counts_ref, fetched_ref, keys_ref, want_ref,
    sums_ref, logsum_ref,
    words, norms, kst, kext, picked, scores, post, acc,
):
    scale = math.log2(math.e) / math.sqrt(feature)

    for s in range(n_slots):
        value = fetched_ref[s]
        scaled = value * scale
        hi = scaled.astype(jnp.bfloat16)
        words[s, :, 0:128] = hi
        words[s, :, 128:256] = (scaled - hi.astype(jnp.float32)).astype(jnp.bfloat16)
        half = (0.5 * scale) * jnp.sum(value * value, axis=1, keepdims=True)
        norms[s] = jnp.broadcast_to(half, (CBLK, 128))
        acc[s] = jnp.zeros((CBLK, 256), jnp.float32)
    kext[:, 128:256] = jnp.ones((block, 128), jnp.bfloat16)

    def key_block(kb, c):
        keys = keys_ref[pl.ds(pl.multiple_of(kb * block, block), block), :]
        kext[:, 0:128] = keys
        turned = jnp.transpose(keys)
        kst[0:128, :] = turned
        kst[128:256, :] = turned
        count = counts_ref[kb]
        slots = [slots_ref[kb, l] for l in range(LIST_MAX)]
        for l in range(LIST_MAX):
            picked[l * CBLK : (l + 1) * CBLK, :] = words[slots[l]]
        raw = jnp.dot(picked[...], kst[...], preferred_element_type=jnp.float32)
        top = jnp.full((8, block), -3e38, jnp.float32)
        for l in range(LIST_MAX):
            rows = slice(l * CBLK, (l + 1) * CBLK)
            less = norms[slots[l]] + jnp.where(l < count, 0.0, 1e30)
            s = raw[rows] - jnp.tile(less, (1, block // 128))
            scores[rows, :] = s
            top = jnp.maximum(top, jnp.max(s.reshape(CBLK // 8, 8, block), axis=0))
        peak = jnp.max(top, axis=0, keepdims=True)
        total = jnp.zeros((8, block), jnp.float32)
        for l in range(LIST_MAX):
            rows = slice(l * CBLK, (l + 1) * CBLK)
            e = jnp.exp2(scores[rows, :] - peak)
            scores[rows, :] = e
            total = total + jnp.sum(e.reshape(CBLK // 8, 8, block), axis=0)
        total = jnp.sum(total, axis=0, keepdims=True)
        logsum_ref[kb] = peak * math.log(2.0) + jnp.log(total)
        inv = 1.0 / total
        post[...] = (scores[...] * inv).astype(jnp.bfloat16)
        weighted = jnp.dot(post[...], kext[...], preferred_element_type=jnp.float32)
        for l in range(LIST_MAX):
            acc[slots[l]] += weighted[l * CBLK : (l + 1) * CBLK]
        return c

    lax.fori_loop(0, key_blocks, key_block, 0)

    for s in range(n_slots):
        sums_ref[s, :CBLK, :] = acc[s, :, 0:128]
        for h in range(2):
            turned = jnp.transpose(acc[s, h * 128 : (h + 1) * 128, 128:256])
            sums_ref[s, CBLK + h : CBLK + h + 1, :] = turned[0:1, :]
        sums_ref[s, CBLK + 2 :, :] = want_ref[s, 2:, :].astype(jnp.float32)


def on_device(cached_keys, codebook, block_lists, counts):
    n_dp = lax.axis_size("dp")
    n_code = lax.axis_size("code")
    n = n_dp * n_code
    own_rows, feature = codebook.shape
    own_blocks = own_rows // CBLK
    key_blocks = block_lists.shape[0]
    block = cached_keys.shape[0] // key_blocks
    f32 = jnp.float32
    dma = pltpu.SemaphoreType.DMA

    slots = block_lists // own_blocks
    local = block_lists % own_blocks
    wanted = jnp.max(
        jnp.where(
            slots.reshape(-1)[:, None] == jnp.arange(128)[None, :], local.reshape(-1)[:, None], 0
        ),
        axis=0,
    )
    want = jnp.broadcast_to(wanted[:n_code, None, None], (n_code, 8, 128)).astype(jnp.int32)
    blocks = jax.ShapeDtypeStruct((n_code, CBLK, feature), f32)
    sums_shape = jax.ShapeDtypeStruct((n_code, CBLK + MROWS, feature), f32)
    con_shape = jax.ShapeDtypeStruct((n, CBLK + MROWS, feature), f32)
    n_y = n_dp // 2

    def params(**kw):
        return pltpu.CompilerParams(vmem_limit_bytes=VLIMIT, **kw)

    book = codebook.reshape(own_blocks, CBLK, feature)
    fetched, served, asked = pl.pallas_call(
        functools.partial(fetch_kernel, n_code),
        out_shape=(blocks, blocks, jax.ShapeDtypeStruct((n_code, 8, 128), jnp.int32)),
        in_specs=[VM, ANY],
        out_specs=(VM, VM, VM),
        scratch_shapes=[
            pltpu.VMEM((own_blocks, CBLK, feature), f32),
            pltpu.SMEM((n_code, 8, 128), jnp.int32),
            dma((n_code,)), dma((n_code,)), dma((n_code,)), dma((n_code,)),
            dma, dma, dma((n_code,)),
        ],
        compiler_params=params(collective_id=0, has_side_effects=True),
    )(want, book)
    logsum = None
    gathered = []
    current = book
    joint = ITERS * n * (CBLK + MROWS) * feature * 4 <= HELD_BYTES

    def finish(parts, held):
        return pl.pallas_call(
            functools.partial(finish_kernel, n, own_blocks, len(parts)),
            out_shape=jax.ShapeDtypeStruct((own_blocks, CBLK, feature), f32),
            in_specs=[ANY] * (len(parts) + 1),
            out_specs=ANY,
            scratch_shapes=[
                pltpu.VMEM(con_shape.shape, f32),
                pltpu.VMEM((own_blocks, CBLK, feature), f32),
                pltpu.VMEM((max(128, 2 * own_blocks), 128), f32),
                pltpu.SMEM((n,), jnp.int32),
                dma((2,)), dma, dma((own_blocks,)),
            ],
            compiler_params=params(),
        )(*parts, held)

    for sweep in range(ITERS):
        sums, logsum = pl.pallas_call(
            functools.partial(assign_kernel, n_code, key_blocks, block, feature),
            out_shape=(sums_shape, jax.ShapeDtypeStruct((key_blocks, 1, block), f32)),
            in_specs=[SM, SM, VM, VM, VM],
            out_specs=(VM, VM),
            scratch_shapes=[
                pltpu.VMEM((n_code, CBLK, 256), jnp.bfloat16),
                pltpu.VMEM((n_code, CBLK, 128), f32),
                pltpu.VMEM((256, block), jnp.bfloat16),
                pltpu.VMEM((block, 256), jnp.bfloat16),
                pltpu.VMEM((LIST_MAX * CBLK, 256), jnp.bfloat16),
                pltpu.VMEM((LIST_MAX * CBLK, block), f32),
                pltpu.VMEM((LIST_MAX * CBLK, block), jnp.bfloat16),
                pltpu.VMEM((n_code, CBLK, 256), f32),
            ],
            compiler_params=params(),
        )(slots, counts, fetched, cached_keys, want)
        reply = sweep + 1 < ITERS
        sems = [
            dma((n_code,)), dma((n_code,)),
            dma((n_y, n_code)), dma((n_y, n_code)),
            dma((n_y, n_code)), dma((n_y, n_code)),
            dma,
        ]
        if reply:
            con, fetched = pl.pallas_call(
                functools.partial(exchange_kernel, n_dp, n_code, True),
                out_shape=(con_shape, blocks),
                in_specs=[VM, VM, VM],
                out_specs=(VM, VM),
                scratch_shapes=[
                    pltpu.VMEM(sums_shape.shape, f32), pltpu.VMEM(blocks.shape, f32)
                ] + sems + [dma((n_code,)), dma((n_code,))],
                compiler_params=params(collective_id=1 + sweep, has_side_effects=True),
            )(sums, served, asked)
        else:
            con = pl.pallas_call(
                functools.partial(exchange_kernel, n_dp, n_code, False),
                out_shape=con_shape,
                in_specs=[VM],
                out_specs=VM,
                scratch_shapes=sems,
                compiler_params=params(collective_id=1 + sweep, has_side_effects=True),
            )(sums)
        gathered.append(con)
        if not joint:
            current = finish(gathered, current)
            gathered = []
            if reply:
                current, fetched = lax.optimization_barrier((current, fetched))
    if gathered:
        current = finish(gathered, current)
    return (current.reshape(own_rows, feature), logsum.reshape(-1))


def solution(mesh):
    in_specs = (
        P(("dp", "code"), None),
        P("code", None),
        P(("dp", "code"), None),
        P(("dp", "code")),
    )
    out_specs = (P("code", None), P(("dp", "code")))
    return jax.shard_map(
        on_device, mesh=mesh, in_specs=in_specs, out_specs=out_specs, check_vma=False
    )
```

```python
import functools
import math

import jax
import jax.numpy as jnp
from jax import lax
from jax.experimental import pallas as pl
from jax.experimental.pallas import tpu as pltpu
from jax.sharding import PartitionSpec as P

CBLK = 256
LIST_MAX = 6
ITERS = 2
MROWS = 8
MESH = pl.DeviceIdType.MESH
VLIMIT = 60 * 1024 * 1024
HELD_BYTES = 16 * 1024 * 1024

VM = pl.BlockSpec(memory_space=pltpu.VMEM)
SM = pl.BlockSpec(memory_space=pltpu.SMEM)
ANY = pl.BlockSpec(memory_space=pl.ANY)


def flip(value, bits):
    out = value
    bit = 1
    while bit <= bits:
        if bits & bit:
            out = out + bit * (1 - 2 * (value // bit % 2))
        bit *= 2
    return out


def remote(src, dst, send, recv, dp, code):
    return pltpu.make_async_remote_copy(
        src_ref=src, dst_ref=dst, send_sem=send, recv_sem=recv,
        device_id=(dp, code), device_id_type=MESH,
    )


def fetch_kernel(
    n_code, want_ref, book_hbm, out_ref, served_ref, asked_ref,
    book, ids, id_send, id_recv, send_sem, recv_sem, book_sem, own_sem, smem_sem,
):
    d = lax.axis_index("dp")
    o = lax.axis_index("code")
    barrier = pltpu.get_barrier_semaphore()
    for k in range(1, n_code):
        pl.semaphore_signal(barrier, inc=1, device_id=(d, flip(o, k)), device_id_type=MESH)
    load = pltpu.make_async_copy(book_hbm, book, book_sem)
    load.start()
    own = pltpu.make_async_copy(want_ref.at[o], asked_ref.at[o], own_sem)
    own.start()
    pl.semaphore_wait(barrier, n_code - 1)
    asks = []
    for k in range(1, n_code):
        peer = flip(o, k)
        copy = remote(
            want_ref.at[peer], asked_ref.at[o], id_send.at[k], id_recv.at[k], d, peer
        )
        copy.start()
        asks.append(copy)
    load.wait()
    copies = []
    for k in range(1, n_code):
        peer = flip(o, k)
        asks[k - 1].wait_recv()
        move = pltpu.make_async_copy(asked_ref.at[peer], ids.at[k], smem_sem.at[k])
        move.start()
        move.wait()
        served_ref[peer] = book[ids[k, 0, 0]]
        copy = remote(
            served_ref.at[peer], out_ref.at[o], send_sem.at[k], recv_sem.at[k], d, peer
        )
        copy.start()
        copies.append(copy)
    own.wait()
    move = pltpu.make_async_copy(asked_ref.at[o], ids.at[0], smem_sem.at[0])
    move.start()
    move.wait()
    block = book[ids[0, 0, 0]]
    served_ref[o] = block
    out_ref[o] = block
    for ask in asks:
        ask.wait_send()
    for copy in copies:
        copy.wait()


def exchange_kernel(n_dp, n_code, reply, *refs):
    if reply:
        (sums_ref, served_ref, asked_ref, con_ref, back_ref, acc, stage,
         a_send, a_recv, y_send, y_recv, c_send, c_recv, own_sem, b_send, b_recv) = refs
    else:
        (sums_ref, con_ref,
         a_send, a_recv, y_send, y_recv, c_send, c_recv, own_sem) = refs
    d = lax.axis_index("dp")
    o = lax.axis_index("code")
    n_y = n_dp // 2
    y = d // 2
    core = d % 2
    mate = y * 2 + 1 - core
    barrier = pltpu.get_barrier_semaphore()
    for k in range(1, n_code):
        pl.semaphore_signal(barrier, inc=1, device_id=(d, flip(o, k)), device_id_type=MESH)
    for j in range(1, n_y):
        pl.semaphore_signal(
            barrier, inc=1, device_id=((y + j) % n_y * 2 + core, o), device_id_type=MESH
        )
    pl.semaphore_signal(barrier, inc=1, device_id=(mate, o), device_id_type=MESH)
    own = pltpu.make_async_copy(sums_ref.at[o], con_ref.at[d * n_code + o], own_sem)
    own.start()
    pl.semaphore_wait(barrier, n_code - 1 + n_y - 1 + 1)

    sends = []
    across = []
    for k in range(1, n_code):
        peer = flip(o, k)
        copy = remote(
            sums_ref.at[peer], con_ref.at[d * n_code + o], a_send.at[k], a_recv.at[k], d, peer
        )
        copy.start()
        across.append(copy)
        sends.append(copy)

    def to_y(k, j):
        row = d * n_code + flip(o, k)
        return remote(
            con_ref.at[row], con_ref.at[row], y_send.at[j, k], y_recv.at[j, k],
            (y + j) % n_y * 2 + core, o,
        )

    def held(k, j):
        return ((y + n_y - j) % n_y * 2 + core) * n_code + flip(o, k)

    def to_mate(k, j):
        row = held(k, j)
        return remote(
            con_ref.at[row], con_ref.at[row], c_send.at[j, k], c_recv.at[j, k], mate, o
        )

    if reply:
        acc[...] = jnp.zeros_like(acc)

    def absorb(row):
        if not reply:
            return
        here = con_ref[row, pl.ds(CBLK + 2, 1), :]

        def one(i, c):
            same = (asked_ref[i, pl.ds(0, 1), :].astype(jnp.float32) == here).astype(jnp.float32)
            acc[i] += con_ref[row] * same
            return c

        lax.fori_loop(0, n_code, one, 0)

    y_copies = {}
    mates = {}
    for k in range(n_code):
        if k == 0:
            own.wait()
        else:
            across[k - 1].wait_recv()
        for j in range(1, n_y):
            copy = to_y(k, j)
            copy.start()
            y_copies[j, k] = copy
            sends.append(copy)
        copy = to_mate(k, 0)
        copy.start()
        mates[0, k] = copy
        sends.append(copy)
        absorb(held(k, 0))
    for k in range(n_code):
        for j in range(1, n_y):
            y_copies[j, k].wait_recv()
            copy = to_mate(k, j)
            copy.start()
            mates[j, k] = copy
            sends.append(copy)
            absorb(held(k, j))
        mates[0, k].wait_recv()
        absorb(held(k, 0) + (1 - 2 * core) * n_code)
    for k in range(n_code):
        for j in range(1, n_y):
            mates[j, k].wait_recv()
            absorb(held(k, j) + (1 - 2 * core) * n_code)
    if reply:
        backs = []
        for k in range(n_code):
            peer = flip(o, k)
            for h in range(2):
                inv = 1.0 / (acc[peer, pl.ds(CBLK + h, 1), :] + 1.0)
                column = jnp.transpose(jnp.broadcast_to(inv, (128, 128)))
                rows = pl.ds(h * 128, 128)
                fresh = (acc[peer, rows, :] + served_ref[peer, rows, :]) * column
                if k == 0:
                    back_ref[o, rows, :] = fresh
                else:
                    stage[k, rows, :] = fresh
        for k in range(n_code - 1, 0, -1):
            copy = remote(
                stage.at[k], back_ref.at[o], b_send.at[k], b_recv.at[k], d, flip(o, k)
            )
            copy.start()
            backs.append(copy)
        for copy in backs:
            copy.wait()
    for copy in sends:
        copy.wait_send()


def fused_kernel(n_dp, n_code, key_blocks, block, feature, reply, *refs):
    slots_ref, counts_ref, fetched_ref, keys_ref, want_ref = refs[:5]
    refs = refs[5:]
    if reply:
        served_ref, asked_ref, con_ref, logsum_ref, back_ref = refs[:5]
        refs = refs[5:]
        acc, stage, b_send, b_recv = refs[:4]
        refs = refs[4:]
    else:
        con_ref, logsum_ref = refs[:2]
        refs = refs[2:]
    (words, norms, kst, kext, scores, post, sums, part,
     a_send, a_recv, y_send, y_recv, c_send, c_recv, own_sem) = refs
    scale = math.log2(math.e) / math.sqrt(feature)
    d = lax.axis_index("dp")
    o = lax.axis_index("code")
    n_y = n_dp // 2
    y = d // 2
    core = d % 2
    mate = y * 2 + 1 - core
    barrier = pltpu.get_barrier_semaphore()
    for k in range(1, n_code):
        pl.semaphore_signal(barrier, inc=1, device_id=(d, flip(o, k)), device_id_type=MESH)
    for j in range(1, n_y):
        pl.semaphore_signal(
            barrier, inc=1, device_id=((y + j) % n_y * 2 + core, o), device_id_type=MESH
        )
    pl.semaphore_signal(barrier, inc=1, device_id=(mate, o), device_id_type=MESH)

    def prepare(s, c):
        value = fetched_ref[s]
        scaled = value * scale
        hi = scaled.astype(jnp.bfloat16)
        words[s, :, 0:128] = hi
        words[s, :, 128:256] = (scaled - hi.astype(jnp.float32)).astype(jnp.bfloat16)
        half = (0.5 * scale) * jnp.sum(value * value, axis=1, keepdims=True)
        norms[s] = jnp.broadcast_to(half, (CBLK, 128))
        return c

    lax.fori_loop(0, n_code, prepare, 0)
    kext[:, 0:128] = keys_ref[...]
    kext[:, 128:256] = jnp.ones((key_blocks * block, 128), jnp.bfloat16)
    post[key_blocks * LIST_MAX] = jnp.zeros((CBLK, block), jnp.bfloat16)

    def key_block(kb, c):
        keys = keys_ref[pl.ds(pl.multiple_of(kb * block, block), block), :]
        turned = jnp.transpose(keys)
        kst[0:128, :] = turned
        kst[128:256, :] = turned
        count = counts_ref[kb]
        slots = [slots_ref[kb, l] for l in range(LIST_MAX)]
        picked = jnp.concatenate([words[slots[l]] for l in range(LIST_MAX)], axis=0)
        raw = jnp.dot(picked, kst[...], preferred_element_type=jnp.float32)
        top = jnp.full((8, block), -3e38, jnp.float32)
        for l in range(LIST_MAX):
            rows = slice(l * CBLK, (l + 1) * CBLK)
            less = norms[slots[l]] + jnp.where(l < count, 0.0, 1e30)
            s = raw[rows] - jnp.tile(less, (1, block // 128))
            scores[rows, :] = s
            top = jnp.maximum(top, jnp.max(s.reshape(CBLK // 8, 8, block), axis=0))
        peak = jnp.max(top, axis=0, keepdims=True)
        total = jnp.zeros((8, block), jnp.float32)
        for l in range(LIST_MAX):
            rows = slice(l * CBLK, (l + 1) * CBLK)
            e = jnp.exp2(scores[rows, :] - peak)
            scores[rows, :] = e
            total = total + jnp.sum(e.reshape(CBLK // 8, 8, block), axis=0)
        total = jnp.sum(total, axis=0, keepdims=True)
        logsum_ref[kb] = peak * math.log(2.0) + jnp.log(total)
        inv = 1.0 / total
        for l in range(LIST_MAX):
            rows = slice(l * CBLK, (l + 1) * CBLK)
            post[kb * LIST_MAX + l] = (scores[rows, :] * inv).astype(jnp.bfloat16)
        return c

    lax.fori_loop(0, key_blocks, key_block, 0)

    def collect(slot):
        for kb in range(key_blocks):
            entry = key_blocks * LIST_MAX
            for l in range(LIST_MAX):
                hit = (slots_ref[kb, l] == slot) & (counts_ref[kb] > l)
                entry = jnp.where(hit, kb * LIST_MAX + l, entry)
            piece = jnp.dot(
                post[entry], kext[kb * block : (kb + 1) * block, :],
                preferred_element_type=jnp.float32,
            )
            if kb == 0:
                part[...] = piece
            else:
                part[...] += piece
        for h in range(2):
            turned = jnp.transpose(part[h * 128 : (h + 1) * 128, 128:256])
            sums[slot, CBLK + h : CBLK + h + 1, :] = turned[0:1, :]
        sums[slot, CBLK + 2 :, :] = want_ref[slot, 2:, :].astype(jnp.float32)
        sums[slot, :CBLK, :] = part[:, 0:128]

    def turn(k):
        out = o
        bit = 1
        while bit < n_code:
            out = out + bit * (k // bit % 2) * (1 - 2 * (o // bit % 2))
            bit *= 2
        return out

    def across(k):
        peer = turn(k)
        return remote(
            sums.at[peer], con_ref.at[d * n_code + o], a_send.at[k], a_recv.at[k], d, peer
        )

    far = n_code // 2
    collect(turn(far))
    pl.semaphore_wait(barrier, n_code - 1 + n_y - 1 + 1)

    def step(k, c):
        collect(turn(k))
        across(k - 1).start()
        return c

    lax.fori_loop(far + 1, n_code, step, 0)
    collect(o)
    across(n_code - 1).start()
    own = pltpu.make_async_copy(sums.at[o], con_ref.at[d * n_code + o], own_sem)
    own.start()

    def held(k, j):
        return ((y + n_y - j) % n_y * 2 + core) * n_code + flip(o, k)

    sends = []

    def to_y(k, j):
        row = held(k, 0)
        copy = remote(
            con_ref.at[row], con_ref.at[row], y_send.at[j, k], y_recv.at[j, k],
            (y + j) % n_y * 2 + core, o,
        )
        copy.start()
        sends.append(copy)
        return copy

    def to_mate(k, j):
        row = held(k, j)
        copy = remote(
            con_ref.at[row], con_ref.at[row], c_send.at[j, k], c_recv.at[j, k], mate, o
        )
        copy.start()
        sends.append(copy)
        return copy

    if reply:
        acc[...] = jnp.zeros_like(acc)

    def absorb(row):
        if not reply:
            return
        here = con_ref[row, pl.ds(CBLK + 2, 1), :]

        def one(i, c):
            same = (asked_ref[i, pl.ds(0, 1), :].astype(jnp.float32) == here).astype(jnp.float32)
            acc[i] += con_ref[row] * same
            return c

        lax.fori_loop(0, n_code, one, 0)

    y_copies = {}
    mates = {}
    own.wait()
    for j in range(1, n_y):
        y_copies[j, 0] = to_y(0, j)
    mates[0, 0] = to_mate(0, 0)

    def near(k, c):
        collect(turn(k))

        @pl.when(k > 1)
        def _():
            across(k - 1).start()

        return c

    lax.fori_loop(1, far, near, 0)
    absorb(held(0, 0))
    across(far - 1).start()

    for k in range(1, n_code):
        across(k).wait_recv()
        for j in range(1, n_y):
            y_copies[j, k] = to_y(k, j)
        mates[0, k] = to_mate(k, 0)
        absorb(held(k, 0))
    for k in range(n_code):
        for j in range(1, n_y):
            y_copies[j, k].wait_recv()
            mates[j, k] = to_mate(k, j)
            absorb(held(k, j))
        mates[0, k].wait_recv()
        absorb(held(k, 0) + (1 - 2 * core) * n_code)
    for k in range(n_code):
        for j in range(1, n_y):
            mates[j, k].wait_recv()
            absorb(held(k, j) + (1 - 2 * core) * n_code)
    if reply:
        order = list(range(far, n_code)) + list(range(1, far))
        for k in order + [0]:
            peer = flip(o, k)
            for h in range(2):
                inv = 1.0 / (acc[peer, pl.ds(CBLK + h, 1), :] + 1.0)
                column = jnp.transpose(jnp.broadcast_to(inv, (128, 128)))
                rows = pl.ds(h * 128, 128)
                fresh = (acc[peer, rows, :] + served_ref[peer, rows, :]) * column
                if k == 0:
                    back_ref[o, rows, :] = fresh
                else:
                    stage[k, rows, :] = fresh
        backs = []
        for k in order:
            copy = remote(
                stage.at[k], back_ref.at[o], b_send.at[k], b_recv.at[k], d, flip(o, k)
            )
            copy.start()
            backs.append(copy)
        for copy in backs:
            copy.wait()
    for k in range(1, n_code):
        across(k).wait_send()
    for copy in sends:
        copy.wait_send()


def finish_kernel(n, own_blocks, sweeps, *refs):
    con_hbm = refs[:sweeps]
    book_hbm, out_hbm = refs[sweeps : sweeps + 2]
    con, total, mass, ids, con_sem, book_sem, out_sem = refs[sweeps + 2 :]
    book = pltpu.make_async_copy(book_hbm, total, book_sem)
    book.start()
    half = n // 2

    def load(t, h):
        rows = pl.ds(h * half, half)
        return pltpu.make_async_copy(con_hbm[t].at[rows], con.at[rows], con_sem.at[h])

    load(0, 0).start()
    load(0, 1).start()
    outs = []
    for t in range(sweeps):
        mass[...] = jnp.ones_like(mass)
        for h in range(2):
            load(t, h).wait()
            if t == 0:

                def name(j, c):
                    for u in range(4):
                        i = j * 4 + u
                        ids[i] = jnp.max(con[i, pl.ds(CBLK + 2, 1), :]).astype(jnp.int32)
                    return c

                lax.fori_loop(h * half // 4, (h + 1) * half // 4, name, 0)
                if h == 0:
                    book.wait()

            def add(j, c):
                b = ids[j]
                total[b] += con[j, :CBLK, :]
                for g in range(2):
                    row = pl.ds(g * (mass.shape[0] // 2) + b, 1)
                    mass[row, :] += con[j, pl.ds(CBLK + g, 1), :]
                return c

            lax.fori_loop(h * half, (h + 1) * half, add, 0)
            if t + 1 < sweeps:
                load(t + 1, h).start()
        columns = jnp.transpose(1.0 / mass[...])
        for b in range(own_blocks):
            for g in range(2):
                lane = g * (mass.shape[0] // 2) + b
                total[b, g * 128 : (g + 1) * 128, :] = (
                    total[b, g * 128 : (g + 1) * 128, :] * columns[:, lane : lane + 1]
                )
            if t + 1 == sweeps:
                out = pltpu.make_async_copy(total.at[b], out_hbm.at[b], out_sem.at[b])
                out.start()
                outs.append(out)
    for out in outs:
        out.wait()


def assign_kernel(
    n_slots, key_blocks, block, feature,
    slots_ref, counts_ref, fetched_ref, keys_ref, want_ref,
    sums_ref, logsum_ref,
    words, norms, kst, kext, picked, scores, post, acc,
):
    scale = math.log2(math.e) / math.sqrt(feature)

    for s in range(n_slots):
        value = fetched_ref[s]
        scaled = value * scale
        hi = scaled.astype(jnp.bfloat16)
        words[s, :, 0:128] = hi
        words[s, :, 128:256] = (scaled - hi.astype(jnp.float32)).astype(jnp.bfloat16)
        half = (0.5 * scale) * jnp.sum(value * value, axis=1, keepdims=True)
        norms[s] = jnp.broadcast_to(half, (CBLK, 128))
        acc[s] = jnp.zeros((CBLK, 256), jnp.float32)
    kext[:, 128:256] = jnp.ones((block, 128), jnp.bfloat16)

    def key_block(kb, c):
        keys = keys_ref[pl.ds(pl.multiple_of(kb * block, block), block), :]
        kext[:, 0:128] = keys
        turned = jnp.transpose(keys)
        kst[0:128, :] = turned
        kst[128:256, :] = turned
        count = counts_ref[kb]
        slots = [slots_ref[kb, l] for l in range(LIST_MAX)]
        for l in range(LIST_MAX):
            picked[l * CBLK : (l + 1) * CBLK, :] = words[slots[l]]
        raw = jnp.dot(picked[...], kst[...], preferred_element_type=jnp.float32)
        top = jnp.full((8, block), -3e38, jnp.float32)
        for l in range(LIST_MAX):
            rows = slice(l * CBLK, (l + 1) * CBLK)
            less = norms[slots[l]] + jnp.where(l < count, 0.0, 1e30)
            s = raw[rows] - jnp.tile(less, (1, block // 128))
            scores[rows, :] = s
            top = jnp.maximum(top, jnp.max(s.reshape(CBLK // 8, 8, block), axis=0))
        peak = jnp.max(top, axis=0, keepdims=True)
        total = jnp.zeros((8, block), jnp.float32)
        for l in range(LIST_MAX):
            rows = slice(l * CBLK, (l + 1) * CBLK)
            e = jnp.exp2(scores[rows, :] - peak)
            scores[rows, :] = e
            total = total + jnp.sum(e.reshape(CBLK // 8, 8, block), axis=0)
        total = jnp.sum(total, axis=0, keepdims=True)
        logsum_ref[kb] = peak * math.log(2.0) + jnp.log(total)
        inv = 1.0 / total
        post[...] = (scores[...] * inv).astype(jnp.bfloat16)
        weighted = jnp.dot(post[...], kext[...], preferred_element_type=jnp.float32)
        for l in range(LIST_MAX):
            acc[slots[l]] += weighted[l * CBLK : (l + 1) * CBLK]
        return c

    lax.fori_loop(0, key_blocks, key_block, 0)

    for s in range(n_slots):
        sums_ref[s, :CBLK, :] = acc[s, :, 0:128]
        for h in range(2):
            turned = jnp.transpose(acc[s, h * 128 : (h + 1) * 128, 128:256])
            sums_ref[s, CBLK + h : CBLK + h + 1, :] = turned[0:1, :]
        sums_ref[s, CBLK + 2 :, :] = want_ref[s, 2:, :].astype(jnp.float32)


def on_device(cached_keys, codebook, block_lists, counts):
    n_dp = lax.axis_size("dp")
    n_code = lax.axis_size("code")
    n = n_dp * n_code
    own_rows, feature = codebook.shape
    own_blocks = own_rows // CBLK
    key_blocks = block_lists.shape[0]
    block = cached_keys.shape[0] // key_blocks
    f32 = jnp.float32
    dma = pltpu.SemaphoreType.DMA

    slots = block_lists // own_blocks
    local = block_lists % own_blocks
    wanted = jnp.max(
        jnp.where(
            slots.reshape(-1)[:, None] == jnp.arange(128)[None, :], local.reshape(-1)[:, None], 0
        ),
        axis=0,
    )
    want = jnp.broadcast_to(wanted[:n_code, None, None], (n_code, 8, 128)).astype(jnp.int32)
    blocks = jax.ShapeDtypeStruct((n_code, CBLK, feature), f32)
    sums_shape = jax.ShapeDtypeStruct((n_code, CBLK + MROWS, feature), f32)
    con_shape = jax.ShapeDtypeStruct((n, CBLK + MROWS, feature), f32)
    n_y = n_dp // 2

    def params(**kw):
        return pltpu.CompilerParams(vmem_limit_bytes=VLIMIT, **kw)

    book = codebook.reshape(own_blocks, CBLK, feature)
    fetched, served, asked = pl.pallas_call(
        functools.partial(fetch_kernel, n_code),
        out_shape=(blocks, blocks, jax.ShapeDtypeStruct((n_code, 8, 128), jnp.int32)),
        in_specs=[VM, ANY],
        out_specs=(VM, VM, VM),
        scratch_shapes=[
            pltpu.VMEM((own_blocks, CBLK, feature), f32),
            pltpu.SMEM((n_code, 8, 128), jnp.int32),
            dma((n_code,)), dma((n_code,)), dma((n_code,)), dma((n_code,)),
            dma, dma, dma((n_code,)),
        ],
        compiler_params=params(collective_id=0, has_side_effects=True),
    )(want, book)
    logsum = None
    gathered = []
    current = book
    joint = ITERS * n * (CBLK + MROWS) * feature * 4 <= HELD_BYTES

    def finish(parts, held):
        return pl.pallas_call(
            functools.partial(finish_kernel, n, own_blocks, len(parts)),
            out_shape=jax.ShapeDtypeStruct((own_blocks, CBLK, feature), f32),
            in_specs=[ANY] * (len(parts) + 1),
            out_specs=ANY,
            scratch_shapes=[
                pltpu.VMEM(con_shape.shape, f32),
                pltpu.VMEM((own_blocks, CBLK, feature), f32),
                pltpu.VMEM((max(128, 2 * own_blocks), 128), f32),
                pltpu.SMEM((n,), jnp.int32),
                dma((2,)), dma, dma((own_blocks,)),
            ],
            compiler_params=params(),
        )(*parts, held)

    for sweep in range(ITERS):
        reply = sweep + 1 < ITERS
        sems = [
            dma((n_code,)), dma((n_code,)),
            dma((n_y, n_code)), dma((n_y, n_code)),
            dma((n_y, n_code)), dma((n_y, n_code)),
            dma,
        ]
        if joint:
            ins = [slots, counts, fetched, cached_keys, want]
            outs = [con_shape, jax.ShapeDtypeStruct((key_blocks, 1, block), f32)]
            scratch = []
            if reply:
                ins += [served, asked]
                outs += [blocks]
                scratch = [
                    pltpu.VMEM(sums_shape.shape, f32), pltpu.VMEM(blocks.shape, f32),
                    dma((n_code,)), dma((n_code,)),
                ]
            scratch += [
                pltpu.VMEM((n_code, CBLK, 256), jnp.bfloat16),
                pltpu.VMEM((n_code, CBLK, 128), f32),
                pltpu.VMEM((256, block), jnp.bfloat16),
                pltpu.VMEM((key_blocks * block, 256), jnp.bfloat16),
                pltpu.VMEM((LIST_MAX * CBLK, block), f32),
                pltpu.VMEM((key_blocks * LIST_MAX + 1, CBLK, block), jnp.bfloat16),
                pltpu.VMEM(sums_shape.shape, f32),
                pltpu.VMEM((CBLK, 256), f32),
            ] + sems
            results = pl.pallas_call(
                functools.partial(
                    fused_kernel, n_dp, n_code, key_blocks, block, feature, reply
                ),
                out_shape=tuple(outs),
                in_specs=[SM, SM] + [VM] * (len(ins) - 2),
                out_specs=(VM,) * len(outs),
                scratch_shapes=scratch,
                compiler_params=params(collective_id=1 + sweep, has_side_effects=True),
            )(*ins)
            con, logsum = results[:2]
            if reply:
                fetched = results[2]
        else:
            sums, logsum = pl.pallas_call(
                functools.partial(assign_kernel, n_code, key_blocks, block, feature),
                out_shape=(sums_shape, jax.ShapeDtypeStruct((key_blocks, 1, block), f32)),
                in_specs=[SM, SM, VM, VM, VM],
                out_specs=(VM, VM),
                scratch_shapes=[
                    pltpu.VMEM((n_code, CBLK, 256), jnp.bfloat16),
                    pltpu.VMEM((n_code, CBLK, 128), f32),
                    pltpu.VMEM((256, block), jnp.bfloat16),
                    pltpu.VMEM((block, 256), jnp.bfloat16),
                    pltpu.VMEM((LIST_MAX * CBLK, 256), jnp.bfloat16),
                    pltpu.VMEM((LIST_MAX * CBLK, block), f32),
                    pltpu.VMEM((LIST_MAX * CBLK, block), jnp.bfloat16),
                    pltpu.VMEM((n_code, CBLK, 256), f32),
                ],
                compiler_params=params(),
            )(slots, counts, fetched, cached_keys, want)
            if reply:
                con, fetched = pl.pallas_call(
                    functools.partial(exchange_kernel, n_dp, n_code, True),
                    out_shape=(con_shape, blocks),
                    in_specs=[VM, VM, VM],
                    out_specs=(VM, VM),
                    scratch_shapes=[
                        pltpu.VMEM(sums_shape.shape, f32), pltpu.VMEM(blocks.shape, f32)
                    ] + sems + [dma((n_code,)), dma((n_code,))],
                    compiler_params=params(collective_id=1 + sweep, has_side_effects=True),
                )(sums, served, asked)
            else:
                con = pl.pallas_call(
                    functools.partial(exchange_kernel, n_dp, n_code, False),
                    out_shape=con_shape,
                    in_specs=[VM],
                    out_specs=VM,
                    scratch_shapes=sems,
                    compiler_params=params(collective_id=1 + sweep, has_side_effects=True),
                )(sums)
        gathered.append(con)
        if not joint:
            current = finish(gathered, current)
            gathered = []
            if reply:
                current, fetched = lax.optimization_barrier((current, fetched))
    if gathered:
        current = finish(gathered, current)
    return (current.reshape(own_rows, feature), logsum.reshape(-1))


def solution(mesh):
    in_specs = (
        P(("dp", "code"), None),
        P("code", None),
        P(("dp", "code"), None),
        P(("dp", "code")),
    )
    out_specs = (P("code", None), P(("dp", "code")))
    return jax.shard_map(
        on_device, mesh=mesh, in_specs=in_specs, out_specs=out_specs, check_vma=False
    )
```

```python
import functools
import math

import jax
import jax.numpy as jnp
from jax import lax
from jax.experimental import pallas as pl
from jax.experimental.pallas import tpu as pltpu
from jax.sharding import PartitionSpec as P

CBLK = 256
LIST_MAX = 6
ITERS = 2
MROWS = 8
MESH = pl.DeviceIdType.MESH
VLIMIT = 60 * 1024 * 1024
HELD_BYTES = 16 * 1024 * 1024

VM = pl.BlockSpec(memory_space=pltpu.VMEM)
SM = pl.BlockSpec(memory_space=pltpu.SMEM)
ANY = pl.BlockSpec(memory_space=pl.ANY)


def flip(value, bits):
    out = value
    bit = 1
    while bit <= bits:
        if bits & bit:
            out = out + bit * (1 - 2 * (value // bit % 2))
        bit *= 2
    return out


def remote(src, dst, send, recv, dp, code):
    return pltpu.make_async_remote_copy(
        src_ref=src, dst_ref=dst, send_sem=send, recv_sem=recv,
        device_id=(dp, code), device_id_type=MESH,
    )


def fetch_kernel(
    n_code, want_ref, book_hbm, out_ref, served_ref, asked_ref,
    book, ids, id_send, id_recv, send_sem, recv_sem, book_sem, own_sem, smem_sem,
):
    d = lax.axis_index("dp")
    o = lax.axis_index("code")
    barrier = pltpu.get_barrier_semaphore()
    for k in range(1, n_code):
        pl.semaphore_signal(barrier, inc=1, device_id=(d, flip(o, k)), device_id_type=MESH)
    load = pltpu.make_async_copy(book_hbm, book, book_sem)
    load.start()
    own = pltpu.make_async_copy(want_ref.at[o], asked_ref.at[o], own_sem)
    own.start()
    pl.semaphore_wait(barrier, n_code - 1)
    asks = []
    for k in range(1, n_code):
        peer = flip(o, k)
        copy = remote(
            want_ref.at[peer], asked_ref.at[o], id_send.at[k], id_recv.at[k], d, peer
        )
        copy.start()
        asks.append(copy)
    load.wait()
    moves = []
    own.wait()
    for k in range(n_code):
        if k > 0:
            asks[k - 1].wait_recv()
        move = pltpu.make_async_copy(asked_ref.at[flip(o, k)], ids.at[k], smem_sem.at[k])
        move.start()
        moves.append(move)
    for move in moves:
        move.wait()
    order = list(range(n_code // 2, n_code)) + list(range(n_code // 2))
    for k in order:
        block = book[ids[k, 0, 0]]
        served_ref[flip(o, k)] = block
        if k == 0:
            out_ref[o] = block
    copies = []
    for k in order:
        if k > 0:
            peer = flip(o, k)
            copy = remote(
                served_ref.at[peer], out_ref.at[o], send_sem.at[k], recv_sem.at[k], d, peer
            )
            copy.start()
            copies.append(copy)
    for ask in asks:
        ask.wait_send()
    for copy in copies:
        copy.wait()


def exchange_kernel(n_dp, n_code, reply, *refs):
    if reply:
        (sums_ref, served_ref, asked_ref, con_ref, back_ref, acc, stage,
         a_send, a_recv, y_send, y_recv, c_send, c_recv, own_sem, b_send, b_recv) = refs
    else:
        (sums_ref, con_ref,
         a_send, a_recv, y_send, y_recv, c_send, c_recv, own_sem) = refs
    d = lax.axis_index("dp")
    o = lax.axis_index("code")
    n_y = n_dp // 2
    y = d // 2
    core = d % 2
    mate = y * 2 + 1 - core
    barrier = pltpu.get_barrier_semaphore()
    for k in range(1, n_code):
        pl.semaphore_signal(barrier, inc=1, device_id=(d, flip(o, k)), device_id_type=MESH)
    for j in range(1, n_y):
        pl.semaphore_signal(
            barrier, inc=1, device_id=((y + j) % n_y * 2 + core, o), device_id_type=MESH
        )
    pl.semaphore_signal(barrier, inc=1, device_id=(mate, o), device_id_type=MESH)
    own = pltpu.make_async_copy(sums_ref.at[o], con_ref.at[d * n_code + o], own_sem)
    own.start()
    pl.semaphore_wait(barrier, n_code - 1 + n_y - 1 + 1)

    sends = []
    across = []
    for k in range(1, n_code):
        peer = flip(o, k)
        copy = remote(
            sums_ref.at[peer], con_ref.at[d * n_code + o], a_send.at[k], a_recv.at[k], d, peer
        )
        copy.start()
        across.append(copy)
        sends.append(copy)

    def to_y(k, j):
        row = d * n_code + flip(o, k)
        return remote(
            con_ref.at[row], con_ref.at[row], y_send.at[j, k], y_recv.at[j, k],
            (y + j) % n_y * 2 + core, o,
        )

    def held(k, j):
        return ((y + n_y - j) % n_y * 2 + core) * n_code + flip(o, k)

    def to_mate(k, j):
        row = held(k, j)
        return remote(
            con_ref.at[row], con_ref.at[row], c_send.at[j, k], c_recv.at[j, k], mate, o
        )

    if reply:
        acc[...] = jnp.zeros_like(acc)

    def absorb(row):
        if not reply:
            return
        here = con_ref[row, pl.ds(CBLK + 2, 1), :]

        def one(i, c):
            same = (asked_ref[i, pl.ds(0, 1), :].astype(jnp.float32) == here).astype(jnp.float32)
            acc[i] += con_ref[row] * same
            return c

        lax.fori_loop(0, n_code, one, 0)

    y_copies = {}
    mates = {}
    for k in range(n_code):
        if k == 0:
            own.wait()
        else:
            across[k - 1].wait_recv()
        for j in range(1, n_y):
            copy = to_y(k, j)
            copy.start()
            y_copies[j, k] = copy
            sends.append(copy)
        copy = to_mate(k, 0)
        copy.start()
        mates[0, k] = copy
        sends.append(copy)
        absorb(held(k, 0))
    for k in range(n_code):
        for j in range(1, n_y):
            y_copies[j, k].wait_recv()
            copy = to_mate(k, j)
            copy.start()
            mates[j, k] = copy
            sends.append(copy)
            absorb(held(k, j))
        mates[0, k].wait_recv()
        absorb(held(k, 0) + (1 - 2 * core) * n_code)
    for k in range(n_code):
        for j in range(1, n_y):
            mates[j, k].wait_recv()
            absorb(held(k, j) + (1 - 2 * core) * n_code)
    if reply:
        backs = []
        for k in range(n_code):
            peer = flip(o, k)
            for h in range(2):
                inv = 1.0 / (acc[peer, pl.ds(CBLK + h, 1), :] + 1.0)
                column = jnp.transpose(jnp.broadcast_to(inv, (128, 128)))
                rows = pl.ds(h * 128, 128)
                fresh = (acc[peer, rows, :] + served_ref[peer, rows, :]) * column
                if k == 0:
                    back_ref[o, rows, :] = fresh
                else:
                    stage[k, rows, :] = fresh
        for k in range(n_code - 1, 0, -1):
            copy = remote(
                stage.at[k], back_ref.at[o], b_send.at[k], b_recv.at[k], d, flip(o, k)
            )
            copy.start()
            backs.append(copy)
        for copy in backs:
            copy.wait()
    for copy in sends:
        copy.wait_send()


def fused_kernel(n_dp, n_code, key_blocks, block, feature, reply, *refs):
    slots_ref, counts_ref, fetched_ref, keys_ref, want_ref = refs[:5]
    refs = refs[5:]
    if reply:
        served_ref, asked_ref, con_ref, logsum_ref, back_ref = refs[:5]
        refs = refs[5:]
        acc, stage, b_send, b_recv = refs[:4]
        refs = refs[4:]
    else:
        con_ref, logsum_ref = refs[:2]
        refs = refs[2:]
    (words, norms, kst, kext, scores, post, sums, part,
     a_send, a_recv, y_send, y_recv, c_send, c_recv, own_sem) = refs
    scale = math.log2(math.e) / math.sqrt(feature)
    d = lax.axis_index("dp")
    o = lax.axis_index("code")
    n_y = n_dp // 2
    y = d // 2
    core = d % 2
    mate = y * 2 + 1 - core
    barrier = pltpu.get_barrier_semaphore()
    for k in range(1, n_code):
        pl.semaphore_signal(barrier, inc=1, device_id=(d, flip(o, k)), device_id_type=MESH)
    for j in range(1, n_y):
        pl.semaphore_signal(
            barrier, inc=1, device_id=((y + j) % n_y * 2 + core, o), device_id_type=MESH
        )
    pl.semaphore_signal(barrier, inc=1, device_id=(mate, o), device_id_type=MESH)

    def prepare(s, c):
        value = fetched_ref[s]
        scaled = value * scale
        hi = scaled.astype(jnp.bfloat16)
        words[s, :, 0:128] = hi
        words[s, :, 128:256] = (scaled - hi.astype(jnp.float32)).astype(jnp.bfloat16)
        half = (0.5 * scale) * jnp.sum(value * value, axis=1, keepdims=True)
        norms[s] = jnp.broadcast_to(half, (CBLK, 128))
        return c

    lax.fori_loop(0, n_code, prepare, 0)
    kext[:, 0:128] = keys_ref[...]
    kext[:, 128:256] = jnp.ones((key_blocks * block, 128), jnp.bfloat16)
    post[key_blocks * LIST_MAX] = jnp.zeros((CBLK, block), jnp.bfloat16)

    def key_block(kb, c):
        keys = keys_ref[pl.ds(pl.multiple_of(kb * block, block), block), :]
        turned = jnp.transpose(keys)
        kst[0:128, :] = turned
        kst[128:256, :] = turned
        count = counts_ref[kb]
        slots = [slots_ref[kb, l] for l in range(LIST_MAX)]
        picked = jnp.concatenate([words[slots[l]] for l in range(LIST_MAX)], axis=0)
        raw = jnp.dot(picked, kst[...], preferred_element_type=jnp.float32)
        top = jnp.full((8, block), -3e38, jnp.float32)
        for l in range(LIST_MAX):
            rows = slice(l * CBLK, (l + 1) * CBLK)
            less = norms[slots[l]] + jnp.where(l < count, 0.0, 1e30)
            s = raw[rows] - jnp.tile(less, (1, block // 128))
            scores[rows, :] = s
            top = jnp.maximum(top, jnp.max(s.reshape(CBLK // 8, 8, block), axis=0))
        peak = jnp.max(top, axis=0, keepdims=True)
        total = jnp.zeros((8, block), jnp.float32)
        for l in range(LIST_MAX):
            rows = slice(l * CBLK, (l + 1) * CBLK)
            e = jnp.exp2(scores[rows, :] - peak)
            scores[rows, :] = e
            total = total + jnp.sum(e.reshape(CBLK // 8, 8, block), axis=0)
        total = jnp.sum(total, axis=0, keepdims=True)
        logsum_ref[kb] = peak * math.log(2.0) + jnp.log(total)
        inv = 1.0 / total
        for l in range(LIST_MAX):
            rows = slice(l * CBLK, (l + 1) * CBLK)
            post[kb * LIST_MAX + l] = (scores[rows, :] * inv).astype(jnp.bfloat16)
        return c

    lax.fori_loop(0, key_blocks, key_block, 0)

    def collect(slot):
        for kb in range(key_blocks):
            entry = key_blocks * LIST_MAX
            for l in range(LIST_MAX):
                hit = (slots_ref[kb, l] == slot) & (counts_ref[kb] > l)
                entry = jnp.where(hit, kb * LIST_MAX + l, entry)
            piece = jnp.dot(
                post[entry], kext[kb * block : (kb + 1) * block, :],
                preferred_element_type=jnp.float32,
            )
            if kb == 0:
                part[...] = piece
            else:
                part[...] += piece
        for h in range(2):
            turned = jnp.transpose(part[h * 128 : (h + 1) * 128, 128:256])
            sums[slot, CBLK + h : CBLK + h + 1, :] = turned[0:1, :]
        sums[slot, CBLK + 2 :, :] = want_ref[slot, 2:, :].astype(jnp.float32)
        sums[slot, :CBLK, :] = part[:, 0:128]

    def turn(k):
        out = o
        bit = 1
        while bit < n_code:
            out = out + bit * (k // bit % 2) * (1 - 2 * (o // bit % 2))
            bit *= 2
        return out

    def across(k):
        peer = turn(k)
        return remote(
            sums.at[peer], con_ref.at[d * n_code + o], a_send.at[k], a_recv.at[k], d, peer
        )

    far = n_code // 2
    collect(o)
    pl.semaphore_wait(barrier, n_code - 1 + n_y - 1 + 1)

    def held(k, j):
        return ((y + n_y - j) % n_y * 2 + core) * n_code + flip(o, k)

    sends = []

    def to_y(k, j):
        row = held(k, 0)
        copy = remote(
            con_ref.at[row], con_ref.at[row], y_send.at[j, k], y_recv.at[j, k],
            (y + j) % n_y * 2 + core, o,
        )
        copy.start()
        sends.append(copy)
        return copy

    def to_mate(k, j):
        row = held(k, j)
        copy = remote(
            con_ref.at[row], con_ref.at[row], c_send.at[j, k], c_recv.at[j, k], mate, o
        )
        copy.start()
        sends.append(copy)
        return copy

    if reply:
        acc[...] = jnp.zeros_like(acc)

    def absorb(row):
        if not reply:
            return
        here = con_ref[row, pl.ds(CBLK + 2, 1), :]

        def one(i, c):
            same = (asked_ref[i, pl.ds(0, 1), :].astype(jnp.float32) == here).astype(jnp.float32)
            acc[i] += con_ref[row] * same
            return c

        lax.fori_loop(0, n_code, one, 0)

    y_copies = {}
    mates = {}
    near = list(range(1, far))
    spread = []
    for k in range(far, n_code):
        spread.append(k)
        if near:
            spread.append(near.pop(0))
    for p, k in enumerate(spread):
        collect(turn(k))
        if p == 0:
            own = pltpu.make_async_copy(sums.at[o], con_ref.at[d * n_code + o], own_sem)
            own.start()
        else:
            across(spread[p - 1]).start()
        if p == 1:
            own.wait()
            for j in range(1, n_y):
                y_copies[j, 0] = to_y(0, j)
            mates[0, 0] = to_mate(0, 0)
    across(spread[-1]).start()
    absorb(held(0, 0))

    for k in range(1, n_code):
        across(k).wait_recv()
        for j in range(1, n_y):
            y_copies[j, k] = to_y(k, j)
        mates[0, k] = to_mate(k, 0)
        absorb(held(k, 0))
    for k in range(n_code):
        for j in range(1, n_y):
            y_copies[j, k].wait_recv()
            mates[j, k] = to_mate(k, j)
            absorb(held(k, j))
        mates[0, k].wait_recv()
        absorb(held(k, 0) + (1 - 2 * core) * n_code)
    for k in range(n_code):
        for j in range(1, n_y):
            mates[j, k].wait_recv()
            absorb(held(k, j) + (1 - 2 * core) * n_code)
    if reply:
        order = list(range(far, n_code)) + list(range(1, far))
        for k in order + [0]:
            peer = flip(o, k)
            for h in range(2):
                inv = 1.0 / (acc[peer, pl.ds(CBLK + h, 1), :] + 1.0)
                column = jnp.transpose(jnp.broadcast_to(inv, (128, 128)))
                rows = pl.ds(h * 128, 128)
                fresh = (acc[peer, rows, :] + served_ref[peer, rows, :]) * column
                if k == 0:
                    back_ref[o, rows, :] = fresh
                else:
                    stage[k, rows, :] = fresh
        backs = []
        for k in order:
            copy = remote(
                stage.at[k], back_ref.at[o], b_send.at[k], b_recv.at[k], d, flip(o, k)
            )
            copy.start()
            backs.append(copy)
        for copy in backs:
            copy.wait()
    for k in range(1, n_code):
        across(k).wait_send()
    for copy in sends:
        copy.wait_send()


def finish_kernel(n, own_blocks, sweeps, *refs):
    con_hbm = refs[:sweeps]
    book_hbm, out_hbm = refs[sweeps : sweeps + 2]
    con, total, mass, ids, con_sem, book_sem, out_sem = refs[sweeps + 2 :]
    book = pltpu.make_async_copy(book_hbm, total, book_sem)
    book.start()
    half = n // 2

    def load(t, h):
        rows = pl.ds(h * half, half)
        return pltpu.make_async_copy(con_hbm[t].at[rows], con.at[rows], con_sem.at[h])

    load(0, 0).start()
    load(0, 1).start()
    outs = []
    for t in range(sweeps):
        mass[...] = jnp.ones_like(mass)
        for h in range(2):
            load(t, h).wait()
            if t == 0:

                def name(j, c):
                    for u in range(4):
                        i = j * 4 + u
                        ids[i] = jnp.max(con[i, pl.ds(CBLK + 2, 1), :]).astype(jnp.int32)
                    return c

                lax.fori_loop(h * half // 4, (h + 1) * half // 4, name, 0)
                if h == 0:
                    book.wait()

            def add(j, c):
                b = ids[j]
                total[b] += con[j, :CBLK, :]
                for g in range(2):
                    row = pl.ds(g * (mass.shape[0] // 2) + b, 1)
                    mass[row, :] += con[j, pl.ds(CBLK + g, 1), :]
                return c

            lax.fori_loop(h * half, (h + 1) * half, add, 0)
            if t + 1 < sweeps:
                load(t + 1, h).start()
        columns = jnp.transpose(1.0 / mass[...])
        for b in range(own_blocks):
            for g in range(2):
                lane = g * (mass.shape[0] // 2) + b
                total[b, g * 128 : (g + 1) * 128, :] = (
                    total[b, g * 128 : (g + 1) * 128, :] * columns[:, lane : lane + 1]
                )
            if t + 1 == sweeps:
                out = pltpu.make_async_copy(total.at[b], out_hbm.at[b], out_sem.at[b])
                out.start()
                outs.append(out)
    for out in outs:
        out.wait()


def assign_kernel(
    n_slots, key_blocks, block, feature,
    slots_ref, counts_ref, fetched_ref, keys_ref, want_ref,
    sums_ref, logsum_ref,
    words, norms, kst, kext, picked, scores, post, acc,
):
    scale = math.log2(math.e) / math.sqrt(feature)

    for s in range(n_slots):
        value = fetched_ref[s]
        scaled = value * scale
        hi = scaled.astype(jnp.bfloat16)
        words[s, :, 0:128] = hi
        words[s, :, 128:256] = (scaled - hi.astype(jnp.float32)).astype(jnp.bfloat16)
        half = (0.5 * scale) * jnp.sum(value * value, axis=1, keepdims=True)
        norms[s] = jnp.broadcast_to(half, (CBLK, 128))
        acc[s] = jnp.zeros((CBLK, 256), jnp.float32)
    kext[:, 128:256] = jnp.ones((block, 128), jnp.bfloat16)

    def key_block(kb, c):
        keys = keys_ref[pl.ds(pl.multiple_of(kb * block, block), block), :]
        kext[:, 0:128] = keys
        turned = jnp.transpose(keys)
        kst[0:128, :] = turned
        kst[128:256, :] = turned
        count = counts_ref[kb]
        slots = [slots_ref[kb, l] for l in range(LIST_MAX)]
        for l in range(LIST_MAX):
            picked[l * CBLK : (l + 1) * CBLK, :] = words[slots[l]]
        raw = jnp.dot(picked[...], kst[...], preferred_element_type=jnp.float32)
        top = jnp.full((8, block), -3e38, jnp.float32)
        for l in range(LIST_MAX):
            rows = slice(l * CBLK, (l + 1) * CBLK)
            less = norms[slots[l]] + jnp.where(l < count, 0.0, 1e30)
            s = raw[rows] - jnp.tile(less, (1, block // 128))
            scores[rows, :] = s
            top = jnp.maximum(top, jnp.max(s.reshape(CBLK // 8, 8, block), axis=0))
        peak = jnp.max(top, axis=0, keepdims=True)
        total = jnp.zeros((8, block), jnp.float32)
        for l in range(LIST_MAX):
            rows = slice(l * CBLK, (l + 1) * CBLK)
            e = jnp.exp2(scores[rows, :] - peak)
            scores[rows, :] = e
            total = total + jnp.sum(e.reshape(CBLK // 8, 8, block), axis=0)
        total = jnp.sum(total, axis=0, keepdims=True)
        logsum_ref[kb] = peak * math.log(2.0) + jnp.log(total)
        inv = 1.0 / total
        post[...] = (scores[...] * inv).astype(jnp.bfloat16)
        weighted = jnp.dot(post[...], kext[...], preferred_element_type=jnp.float32)
        for l in range(LIST_MAX):
            acc[slots[l]] += weighted[l * CBLK : (l + 1) * CBLK]
        return c

    lax.fori_loop(0, key_blocks, key_block, 0)

    for s in range(n_slots):
        sums_ref[s, :CBLK, :] = acc[s, :, 0:128]
        for h in range(2):
            turned = jnp.transpose(acc[s, h * 128 : (h + 1) * 128, 128:256])
            sums_ref[s, CBLK + h : CBLK + h + 1, :] = turned[0:1, :]
        sums_ref[s, CBLK + 2 :, :] = want_ref[s, 2:, :].astype(jnp.float32)


def on_device(cached_keys, codebook, block_lists, counts):
    n_dp = lax.axis_size("dp")
    n_code = lax.axis_size("code")
    n = n_dp * n_code
    own_rows, feature = codebook.shape
    own_blocks = own_rows // CBLK
    key_blocks = block_lists.shape[0]
    block = cached_keys.shape[0] // key_blocks
    f32 = jnp.float32
    dma = pltpu.SemaphoreType.DMA

    slots = block_lists // own_blocks
    local = block_lists % own_blocks
    wanted = jnp.max(
        jnp.where(
            slots.reshape(-1)[:, None] == jnp.arange(128)[None, :], local.reshape(-1)[:, None], 0
        ),
        axis=0,
    )
    want = jnp.broadcast_to(wanted[:n_code, None, None], (n_code, 8, 128)).astype(jnp.int32)
    blocks = jax.ShapeDtypeStruct((n_code, CBLK, feature), f32)
    sums_shape = jax.ShapeDtypeStruct((n_code, CBLK + MROWS, feature), f32)
    con_shape = jax.ShapeDtypeStruct((n, CBLK + MROWS, feature), f32)
    n_y = n_dp // 2

    def params(**kw):
        return pltpu.CompilerParams(vmem_limit_bytes=VLIMIT, **kw)

    book = codebook.reshape(own_blocks, CBLK, feature)
    fetched, served, asked = pl.pallas_call(
        functools.partial(fetch_kernel, n_code),
        out_shape=(blocks, blocks, jax.ShapeDtypeStruct((n_code, 8, 128), jnp.int32)),
        in_specs=[VM, ANY],
        out_specs=(VM, VM, VM),
        scratch_shapes=[
            pltpu.VMEM((own_blocks, CBLK, feature), f32),
            pltpu.SMEM((n_code, 8, 128), jnp.int32),
            dma((n_code,)), dma((n_code,)), dma((n_code,)), dma((n_code,)),
            dma, dma, dma((n_code,)),
        ],
        compiler_params=params(collective_id=0, has_side_effects=True),
    )(want, book)
    logsum = None
    gathered = []
    current = book
    joint = ITERS * n * (CBLK + MROWS) * feature * 4 <= HELD_BYTES

    def finish(parts, held):
        return pl.pallas_call(
            functools.partial(finish_kernel, n, own_blocks, len(parts)),
            out_shape=jax.ShapeDtypeStruct((own_blocks, CBLK, feature), f32),
            in_specs=[ANY] * (len(parts) + 1),
            out_specs=ANY,
            scratch_shapes=[
                pltpu.VMEM(con_shape.shape, f32),
                pltpu.VMEM((own_blocks, CBLK, feature), f32),
                pltpu.VMEM((max(128, 2 * own_blocks), 128), f32),
                pltpu.SMEM((n,), jnp.int32),
                dma((2,)), dma, dma((own_blocks,)),
            ],
            compiler_params=params(),
        )(*parts, held)

    for sweep in range(ITERS):
        reply = sweep + 1 < ITERS
        sems = [
            dma((n_code,)), dma((n_code,)),
            dma((n_y, n_code)), dma((n_y, n_code)),
            dma((n_y, n_code)), dma((n_y, n_code)),
            dma,
        ]
        if joint:
            ins = [slots, counts, fetched, cached_keys, want]
            outs = [con_shape, jax.ShapeDtypeStruct((key_blocks, 1, block), f32)]
            scratch = []
            if reply:
                ins += [served, asked]
                outs += [blocks]
                scratch = [
                    pltpu.VMEM(sums_shape.shape, f32), pltpu.VMEM(blocks.shape, f32),
                    dma((n_code,)), dma((n_code,)),
                ]
            scratch += [
                pltpu.VMEM((n_code, CBLK, 256), jnp.bfloat16),
                pltpu.VMEM((n_code, CBLK, 128), f32),
                pltpu.VMEM((256, block), jnp.bfloat16),
                pltpu.VMEM((key_blocks * block, 256), jnp.bfloat16),
                pltpu.VMEM((LIST_MAX * CBLK, block), f32),
                pltpu.VMEM((key_blocks * LIST_MAX + 1, CBLK, block), jnp.bfloat16),
                pltpu.VMEM(sums_shape.shape, f32),
                pltpu.VMEM((CBLK, 256), f32),
            ] + sems
            results = pl.pallas_call(
                functools.partial(
                    fused_kernel, n_dp, n_code, key_blocks, block, feature, reply
                ),
                out_shape=tuple(outs),
                in_specs=[SM, SM] + [VM] * (len(ins) - 2),
                out_specs=(VM,) * len(outs),
                scratch_shapes=scratch,
                compiler_params=params(collective_id=1 + sweep, has_side_effects=True),
            )(*ins)
            con, logsum = results[:2]
            if reply:
                fetched = results[2]
        else:
            sums, logsum = pl.pallas_call(
                functools.partial(assign_kernel, n_code, key_blocks, block, feature),
                out_shape=(sums_shape, jax.ShapeDtypeStruct((key_blocks, 1, block), f32)),
                in_specs=[SM, SM, VM, VM, VM],
                out_specs=(VM, VM),
                scratch_shapes=[
                    pltpu.VMEM((n_code, CBLK, 256), jnp.bfloat16),
                    pltpu.VMEM((n_code, CBLK, 128), f32),
                    pltpu.VMEM((256, block), jnp.bfloat16),
                    pltpu.VMEM((block, 256), jnp.bfloat16),
                    pltpu.VMEM((LIST_MAX * CBLK, 256), jnp.bfloat16),
                    pltpu.VMEM((LIST_MAX * CBLK, block), f32),
                    pltpu.VMEM((LIST_MAX * CBLK, block), jnp.bfloat16),
                    pltpu.VMEM((n_code, CBLK, 256), f32),
                ],
                compiler_params=params(),
            )(slots, counts, fetched, cached_keys, want)
            if reply:
                con, fetched = pl.pallas_call(
                    functools.partial(exchange_kernel, n_dp, n_code, True),
                    out_shape=(con_shape, blocks),
                    in_specs=[VM, VM, VM],
                    out_specs=(VM, VM),
                    scratch_shapes=[
                        pltpu.VMEM(sums_shape.shape, f32), pltpu.VMEM(blocks.shape, f32)
                    ] + sems + [dma((n_code,)), dma((n_code,))],
                    compiler_params=params(collective_id=1 + sweep, has_side_effects=True),
                )(sums, served, asked)
            else:
                con = pl.pallas_call(
                    functools.partial(exchange_kernel, n_dp, n_code, False),
                    out_shape=con_shape,
                    in_specs=[VM],
                    out_specs=VM,
                    scratch_shapes=sems,
                    compiler_params=params(collective_id=1 + sweep, has_side_effects=True),
                )(sums)
        gathered.append(con)
        if not joint:
            current = finish(gathered, current)
            gathered = []
            if reply:
                current, fetched = lax.optimization_barrier((current, fetched))
    if gathered:
        current = finish(gathered, current)
    return (current.reshape(own_rows, feature), logsum.reshape(-1))


def solution(mesh):
    in_specs = (
        P(("dp", "code"), None),
        P("code", None),
        P(("dp", "code"), None),
        P(("dp", "code")),
    )
    out_specs = (P("code", None), P(("dp", "code")))
    return jax.shard_map(
        on_device, mesh=mesh, in_specs=in_specs, out_specs=out_specs, check_vma=False
    )
```
